32 devices in a mesh: space: 16 (over z, y, core), chan: 2 (over x).
Axes of the slice: x: 2, y: 2, z: 4, core: 2. Of those that a mesh axis runs over, the one named last changes fastest.
Arguments:
- volume: bfloat16 [8, 32, 128, 256], P(None, 'space', None, 'chan'), may hold values from -6 to 6
- first_filter: bfloat16 [3, 3, 3, 256, 256], P(None, None, None, None, 'chan'), may hold values from -0.078125 to 0.078125
- second_filter: bfloat16 [3, 3, 3, 256, 256], P(None, None, None, None, 'chan'), may hold values from -0.078125 to 0.078125
Outputs:
- block_out: bfloat16 [8, 32, 128, 256], P(None, 'space', None, 'chan')
The draws below stay inside these ranges and needn't reach their ends.
All inputs are finite; a program needn't handle non-finite values.
Results may differ from the reference program's by a relative error of at most 0.0032.
Values may be sent and summed in bfloat16 or wider, within the bound.
A program may use at most 128 MiB of HBM per device.

```python
import jax
import jax.numpy as jnp
from jax import lax

C = 256
DEPTH = 8
WIDTH = 128
HEIGHT = 32


def block_levels(stream_key, dims, cuts, low, largest):
    level = 1.0
    for axis_at, blocks in cuts:
        steps = jax.random.uniform(jax.random.fold_in(jax.random.fold_in(stream_key, 6), axis_at), (blocks,), jnp.float32, low / len(cuts), largest / len(cuts))
        level = level * jnp.repeat(jnp.exp(steps), dims[axis_at] // blocks).reshape((-1,) + (1,) * (len(dims) - 1 - axis_at))
    return level


def centred(own_key, extent, spread, reach, shards=(), kind=jnp.bfloat16):
    values = spread * jax.random.normal(own_key, extent, jnp.float32)
    if shards:
        values = values * block_levels(own_key, extent, shards, -0.22, 0.18)
    return jnp.clip(values, -reach, reach).astype(kind)


def setup_inputs(seed: int = 0) -> dict:
    key_list = jax.random.split(jax.random.key(seed), 4)
    return {
        "volume": centred(key_list[0], (DEPTH, HEIGHT, WIDTH, C), 1.0, 6.0, ((1, 16), (3, 2))),
        "first_filter": centred(key_list[1], (3, 3, 3, C, C), (27 * C) ** -0.5, 0.078125, ((4, 2),)),
        "second_filter": centred(key_list[2], (3, 3, 3, C, C), (27 * C) ** -0.5, 0.078125, ((4, 2),)),
    }


def conv(field, filt):
    out = lax.conv_general_dilated(field.astype(jnp.float32)[None], filt.astype(jnp.float32), (1, 1, 1), [(1, 1), (1, 1), (1, 1)], dimension_numbers=("NDHWC", "DHWIO", "NDHWC"), precision=lax.Precision.HIGHEST)
    return out[0]


def reference(volume, first_filter, second_filter):
    hidden = jnp.maximum(conv(volume, first_filter), 0.0).astype(jnp.bfloat16)
    total = volume.astype(jnp.float32) + conv(hidden, second_filter)
    return jnp.maximum(total, 0.0).astype(jnp.bfloat16)
```

```python
import functools

import jax
import jax.numpy as jnp
from jax import lax
from jax.experimental import pallas as pl
from jax.experimental.pallas import tpu as pltpu
from jax.sharding import PartitionSpec as P

MESH = pl.DeviceIdType.MESH
LAG = 5
EARLY = 3
VOLUME, EDGE, CORE, OFF_1, ON_1, OFF_2, ON_2 = range(7)


def shifted(left, middle, right):
    width = middle.shape[-2]
    at = lax.broadcasted_iota(jnp.int32, middle.shape, middle.ndim - 2)
    left = jnp.where(at == 0, 0.0, pltpu.roll(left, 1, middle.ndim - 2))
    right = jnp.where(at == width - 1, 0.0, pltpu.roll(right, width - 1, middle.ndim - 2))
    return left + middle + right


def kernel(
    n_space, volume, first, second, out,
    field, hidden, middle, off_out, off_in, on_out, on_in, w1, w2, local_sem, send_sem, recv_sem,
):
    s, c = lax.axis_index("space"), lax.axis_index("chan")
    depth, planes, width, half = volume.shape
    taps, out_c = first.shape[0], first.shape[4]
    even = lax.rem(s, 2) == 0
    edge = lax.rem(s, 2)
    core = 1 - edge
    has_off = jnp.where(even, s > 0, s < n_space - 1)
    on_dev, off_dev, across = {"space": s + 1 - 2 * edge}, {"space": s - 1 + 2 * edge}, {"chan": 1 - c}

    barrier = pltpu.get_barrier_semaphore()
    pl.semaphore_signal(barrier, inc=1, device_id=across, device_id_type=MESH)
    pl.semaphore_signal(barrier, inc=1, device_id=on_dev, device_id_type=MESH)

    @pl.when(has_off)
    def _():
        pl.semaphore_signal(barrier, inc=1, device_id=off_dev, device_id_type=MESH)

    own_copy = pltpu.make_async_copy(volume, field.at[c, pl.ds(1, depth)], local_sem.at[0])
    own_copy.start()
    filter_copies = []
    for k, (src, dst) in enumerate(((first, w1), (second, w2))):
        for b in range(taps):
            for t in range(taps):
                col = b * taps + t
                filter_copies.append(
                    pltpu.make_async_copy(
                        src.at[:, b, t],
                        dst.at[:, :, pl.ds(col * out_c, out_c)],
                        local_sem.at[1 + taps * taps * k + col],
                    )
                )
    for copy in filter_copies:
        copy.start()

    rim = jnp.zeros((planes, width, half), field.dtype)
    for buf in (field, hidden):
        for h in range(2):
            buf[h, 0] = rim
            buf[h, depth + 1] = rim

    @pl.when(jnp.logical_not(has_off))
    def _():
        off_in[...] = jnp.zeros(off_in.shape, off_in.dtype)

    pl.semaphore_wait(barrier, 2 + has_off.astype(jnp.int32))

    def remote(kind, d):
        if kind == VOLUME:
            src, dst, dev = volume.at[d], field.at[c, d + 1], across
        elif kind in (EDGE, CORE):
            src = hidden.at[c, d + 1, edge if kind == EDGE else core]
            dst, dev = src, across
        elif kind in (OFF_1, OFF_2):
            k = 0 if kind == OFF_1 else 1
            src, dst, dev = off_out.at[k, d], off_in.at[k, d], off_dev
        else:
            k = 0 if kind == ON_1 else 1
            src, dst, dev = on_out.at[k, d], on_in.at[k, d], on_dev
        return pltpu.make_async_remote_copy(
            src_ref=src,
            dst_ref=dst,
            send_sem=send_sem.at[kind, d],
            recv_sem=recv_sem.at[kind, d],
            device_id=dev,
            device_id_type=MESH,
        )

    def repeat(count, body):
        def step(i, carry):
            body(i)
            return carry

        lax.fori_loop(0, count, step, 0)

    repeat(depth, lambda d: remote(VOLUME, d).start())

    def product(rows, w):
        lhs = jnp.concatenate(rows, axis=1)
        w = w[...].reshape(lhs.shape[1], taps * taps * out_c)
        parts = jnp.dot(lhs, w, preferred_element_type=jnp.float32)

        def combine(terms):
            cols = []
            for t in range(taps):
                blocks = [
                    parts[g * width : (g + 1) * width, (b * taps + t) * out_c : (b * taps + t + 1) * out_c]
                    for b, g in terms
                ]
                cols.append(functools.reduce(jnp.add, blocks))
            return shifted(*cols)

        return combine

    def multiply_first(d):
        combine = product(
            [field[h, d + a].reshape(planes * width, half) for a in range(taps) for h in range(2)], w1
        )
        up, down = combine([(0, planes - 1)]), combine([(2, 0)])
        off_out[0, d] = jnp.where(even, down, up).astype(off_out.dtype)
        on_out[0, d] = jnp.where(even, up, down)

        @pl.when(has_off)
        def _():
            remote(OFF_1, d).start()

        remote(ON_1, d).start()
        for p in range(planes):
            middle[d, p] = combine([(b, p + b - 1) for b in range(taps) if 0 <= p + b - 1 < planes])

    def finish_hidden(d):
        @pl.when(has_off)
        def _():
            remote(OFF_1, d).wait_recv()

        total = middle[d, edge] + off_in[0, d].astype(jnp.float32)
        hidden[c, d + 1, edge] = jnp.maximum(total, 0.0).astype(hidden.dtype)
        remote(EDGE, d).start()
        remote(ON_1, d).wait_recv()
        total = middle[d, core] + on_in[0, d]
        hidden[c, d + 1, core] = jnp.maximum(total, 0.0).astype(hidden.dtype)

        @pl.when(d < EARLY)
        def _():
            remote(CORE, d).start()

    def first_step(t):
        @pl.when(t < depth)
        def _():
            remote(VOLUME, t).wait_recv()

        @pl.when(t >= LAG)
        def _():
            finish_hidden(t - LAG)

        @pl.when(jnp.logical_and(t >= 1, t <= depth))
        def _():
            multiply_first(t - 1)

    def plane_product(d, plane):
        return product(
            [
                jnp.concatenate([hidden[h, d + a, plane], hidden[h, d + 1 + a, plane]], axis=0)
                for a in range(taps)
                for h in range(2)
            ],
            w2,
        )

    def await_pair(kind, j):
        @pl.when(j == 0)
        def _():
            remote(kind, 0).wait_recv()

        remote(kind, 2 * j + 1).wait_recv()

        @pl.when(j < depth // 2 - 1)
        def _():
            remote(kind, 2 * j + 2).wait_recv()

    def edge_step(j):
        await_pair(EDGE, j)
        combine = plane_product(2 * j, edge)
        for g in range(2):
            d = 2 * j + g
            below, own, above = combine([(2, g)]), combine([(1, g)]), combine([(0, g)])
            off_out[1, d] = jnp.where(even, below, above).astype(off_out.dtype)

            @pl.when(has_off)
            def _():
                remote(OFF_2, d).start()

            middle[d, edge] = own
            middle[d, core] = jnp.where(even, above, below)

    def core_step(j):
        @pl.when(j < depth // 2)
        def _():
            await_pair(CORE, j)
            combine = plane_product(2 * j, core)
            for g in range(2):
                d = 2 * j + g
                below, own, above = combine([(2, g)]), combine([(1, g)]), combine([(0, g)])
                on_out[1, d] = jnp.where(even, above, below)
                remote(ON_2, d).start()
                middle[d, core] = middle[d, core] + own

                @pl.when(has_off)
                def _():
                    remote(OFF_2, d).wait_recv()

                total = middle[d, edge] + jnp.where(even, below, above) + off_in[1, d].astype(jnp.float32)
                total = total + field[c, d + 1, edge].astype(jnp.float32)
                out[d, edge] = jnp.maximum(total, 0.0).astype(out.dtype)

        @pl.when(j >= 1)
        def _():
            for g in range(2):
                d = 2 * j - 2 + g
                remote(ON_2, d).wait_recv()
                total = middle[d, core] + on_in[1, d] + field[c, d + 1, core].astype(jnp.float32)
                out[d, core] = jnp.maximum(total, 0.0).astype(out.dtype)

    own_copy.wait()
    for copy in filter_copies[: taps * taps]:
        copy.wait()
    repeat(depth + LAG, first_step)
    repeat(depth - EARLY, lambda d: remote(CORE, EARLY + d).start())
    for copy in filter_copies[taps * taps :]:
        copy.wait()
    pairs = depth // 2

    def drain_first(d):
        remote(VOLUME, d).wait_send()
        remote(ON_1, d).wait_send()

        @pl.when(has_off)
        def _():
            remote(OFF_1, d).wait_send()

    repeat(depth, drain_first)

    def second_step(i):
        @pl.when(i < pairs)
        def _():
            edge_step(i)

        @pl.when(i >= pairs)
        def _():
            core_step(i - pairs)

    repeat(2 * pairs + 1, second_step)

    def drain_second(d):
        for kind in (EDGE, CORE, ON_2):
            remote(kind, d).wait_send()

        @pl.when(has_off)
        def _():
            remote(OFF_2, d).wait_send()

    repeat(depth, drain_second)


def per_device(n_space, volume, first_filter, second_filter):
    depth, planes, width, half = volume.shape
    taps, _, _, in_c, out_c = first_filter.shape
    plane_buf = pltpu.VMEM((2, depth + 2, planes, width, half), jnp.bfloat16)
    filter_buf = pltpu.VMEM((taps, in_c, taps * taps * out_c), jnp.bfloat16)
    flops = 2 * 2 * 27 * depth * planes * width * in_c * out_c
    volume, first_filter, second_filter = (
        pltpu.with_memory_space_constraint(x, pltpu.HBM) for x in (volume, first_filter, second_filter)
    )
    return pl.pallas_call(
        functools.partial(kernel, n_space),
        out_shape=pltpu.VMEM(volume.shape, jnp.bfloat16),
        in_specs=[pl.BlockSpec(memory_space=pltpu.HBM)] * 3,
        out_specs=pl.BlockSpec(memory_space=pltpu.VMEM),
        scratch_shapes=[
            plane_buf,
            plane_buf,
            pltpu.VMEM((depth, planes, width, out_c), jnp.float32),
            pltpu.VMEM((2, depth, width, out_c), jnp.bfloat16),
            pltpu.VMEM((2, depth, width, out_c), jnp.bfloat16),
            pltpu.VMEM((2, depth, width, out_c), jnp.float32),
            pltpu.VMEM((2, depth, width, out_c), jnp.float32),
            filter_buf,
            filter_buf,
            pltpu.SemaphoreType.DMA((1 + 2 * taps * taps,)),
            pltpu.SemaphoreType.DMA((7, depth)),
            pltpu.SemaphoreType.DMA((7, depth)),
        ],
        compiler_params=pltpu.CompilerParams(
            collective_id=0, has_side_effects=True, vmem_limit_bytes=40 << 20
        ),
        cost_estimate=pl.CostEstimate(
            flops=flops, bytes_accessed=4 * volume.size + 4 * first_filter.size, transcendentals=0
        ),
    )(volume, first_filter, second_filter)


def solution(mesh):
    return jax.shard_map(
        functools.partial(per_device, mesh.shape["space"]),
        mesh=mesh,
        in_specs=(
            P(None, "space", None, "chan"),
            P(None, None, None, None, "chan"),
            P(None, None, None, None, "chan"),
        ),
        out_specs=P(None, "space", None, "chan"),
        check_vma=False,
    )
```

```python
import functools

import jax
import jax.numpy as jnp
from jax import lax
from jax.experimental import pallas as pl
from jax.experimental.pallas import tpu as pltpu
from jax.sharding import PartitionSpec as P

MESH = pl.DeviceIdType.MESH
LAG = 5
EARLY = 3
VOLUME, EDGE, CORE, OFF_1, ON_1, OFF_2, ON_2 = range(7)


def shifted(left, middle, right):
    width = middle.shape[-2]
    at = lax.broadcasted_iota(jnp.int32, middle.shape, middle.ndim - 2)
    left = jnp.where(at == 0, 0.0, pltpu.roll(left, 1, middle.ndim - 2))
    right = jnp.where(at == width - 1, 0.0, pltpu.roll(right, width - 1, middle.ndim - 2))
    return left + middle + right


def kernel(
    n_space, volume, first, second, out,
    field, hidden, middle, off_out, off_in, on_out, on_in, w1, w2, local_sem, send_sem, recv_sem,
):
    s, c = lax.axis_index("space"), lax.axis_index("chan")
    depth, planes, width, half = volume.shape
    taps, out_c = first.shape[0], first.shape[4]
    even = lax.rem(s, 2) == 0
    edge = lax.rem(s, 2)
    core = 1 - edge
    has_off = jnp.where(even, s > 0, s < n_space - 1)
    on_dev, off_dev, across = {"space": s + 1 - 2 * edge}, {"space": s - 1 + 2 * edge}, {"chan": 1 - c}

    barrier = pltpu.get_barrier_semaphore()
    pl.semaphore_signal(barrier, inc=1, device_id=across, device_id_type=MESH)
    pl.semaphore_signal(barrier, inc=1, device_id=on_dev, device_id_type=MESH)

    @pl.when(has_off)
    def _():
        pl.semaphore_signal(barrier, inc=1, device_id=off_dev, device_id_type=MESH)

    own_copy = pltpu.make_async_copy(volume, field.at[c, pl.ds(1, depth)], local_sem.at[0])
    own_copy.start()
    filter_copies = []
    for k, (src, dst) in enumerate(((first, w1), (second, w2))):
        for b in range(taps):
            for t in range(taps):
                col = b * taps + t
                filter_copies.append(
                    pltpu.make_async_copy(
                        src.at[:, b, t],
                        dst.at[:, :, pl.ds(col * out_c, out_c)],
                        local_sem.at[1 + taps * taps * k + col],
                    )
                )
    for copy in filter_copies:
        copy.start()

    rim = jnp.zeros((planes, width, half), field.dtype)
    for buf in (field, hidden):
        for h in range(2):
            buf[h, 0] = rim
            buf[h, depth + 1] = rim

    @pl.when(jnp.logical_not(has_off))
    def _():
        off_in[...] = jnp.zeros(off_in.shape, off_in.dtype)

    pl.semaphore_wait(barrier, 2 + has_off.astype(jnp.int32))

    def remote(kind, d):
        if kind == VOLUME:
            src, dst, dev = volume.at[d], field.at[c, d + 1], across
        elif kind in (EDGE, CORE):
            src = hidden.at[c, d + 1, edge if kind == EDGE else core]
            dst, dev = src, across
        elif kind in (OFF_1, OFF_2):
            k = 0 if kind == OFF_1 else 1
            src, dst, dev = off_out.at[k, d], off_in.at[k, d], off_dev
        else:
            k = 0 if kind == ON_1 else 1
            src, dst, dev = on_out.at[k, d], on_in.at[k, d], on_dev
        return pltpu.make_async_remote_copy(
            src_ref=src,
            dst_ref=dst,
            send_sem=send_sem.at[kind, d],
            recv_sem=recv_sem.at[kind, d],
            device_id=dev,
            device_id_type=MESH,
        )

    def repeat(count, body):
        def step(i, carry):
            body(i)
            return carry

        lax.fori_loop(0, count, step, 0)

    repeat(depth, lambda d: remote(VOLUME, d).start())

    def product(rows, w):
        lhs = jnp.concatenate(rows, axis=1)
        w = w[...].reshape(lhs.shape[1], taps * taps * out_c)
        parts = jnp.dot(lhs, w, preferred_element_type=jnp.float32)

        def combine(terms):
            cols = []
            for t in range(taps):
                blocks = [
                    parts[g * width : (g + 1) * width, (b * taps + t) * out_c : (b * taps + t + 1) * out_c]
                    for b, g in terms
                ]
                cols.append(functools.reduce(jnp.add, blocks))
            return shifted(*cols)

        return combine

    def multiply_first(d):
        combine = product(
            [field[h, d + a].reshape(planes * width, half) for a in range(taps) for h in range(2)], w1
        )
        up, down = combine([(0, planes - 1)]), combine([(2, 0)])
        off_out[0, d] = jnp.where(even, down, up).astype(off_out.dtype)
        on_out[0, d] = jnp.where(even, up, down)

        @pl.when(has_off)
        def _():
            remote(OFF_1, d).start()

        remote(ON_1, d).start()
        for p in range(planes):
            middle[d, p] = combine([(b, p + b - 1) for b in range(taps) if 0 <= p + b - 1 < planes])

    def finish_hidden(d):
        @pl.when(has_off)
        def _():
            remote(OFF_1, d).wait_recv()

        total = middle[d, edge] + off_in[0, d].astype(jnp.float32)
        hidden[c, d + 1, edge] = jnp.maximum(total, 0.0).astype(hidden.dtype)
        remote(EDGE, d).start()
        remote(ON_1, d).wait_recv()
        total = middle[d, core] + on_in[0, d]
        hidden[c, d + 1, core] = jnp.maximum(total, 0.0).astype(hidden.dtype)

        @pl.when(d < EARLY)
        def _():
            remote(CORE, d).start()

    def first_step(t):
        @pl.when(t < depth)
        def _():
            remote(VOLUME, t).wait_recv()

        @pl.when(t >= LAG)
        def _():
            finish_hidden(t - LAG)

        @pl.when(jnp.logical_and(t >= 1, t <= depth))
        def _():
            multiply_first(t - 1)

    def plane_product(d, plane):
        return product(
            [
                jnp.concatenate([hidden[h, d + a, plane], hidden[h, d + 1 + a, plane]], axis=0)
                for a in range(taps)
                for h in range(2)
            ],
            w2,
        )

    def await_pair(kind, j):
        @pl.when(j == 0)
        def _():
            remote(kind, 0).wait_recv()

        remote(kind, 2 * j + 1).wait_recv()

        @pl.when(j < depth // 2 - 1)
        def _():
            remote(kind, 2 * j + 2).wait_recv()

    def edge_step(j):
        await_pair(EDGE, j)
        combine = plane_product(2 * j, edge)
        for g in range(2):
            d = 2 * j + g
            below, own, above = combine([(2, g)]), combine([(1, g)]), combine([(0, g)])
            off_out[1, d] = jnp.where(even, below, above).astype(off_out.dtype)

            @pl.when(has_off)
            def _():
                remote(OFF_2, d).start()

            middle[d, edge] = own
            middle[d, core] = jnp.where(even, above, below)

    def core_step(j):
        await_pair(CORE, j)
        combine = plane_product(2 * j, core)
        for g in range(2):
            d = 2 * j + g
            below, own, above = combine([(2, g)]), combine([(1, g)]), combine([(0, g)])
            on_out[1, d] = jnp.where(even, above, below)
            remote(ON_2, d).start()
            middle[d, core] = middle[d, core] + own
            middle[d, edge] = middle[d, edge] + jnp.where(even, below, above)

    def finish_pair(j):
        for g in range(2):
            d = 2 * j + g

            @pl.when(has_off)
            def _():
                remote(OFF_2, d).wait_recv()

            total = middle[d, edge] + off_in[1, d].astype(jnp.float32) + field[c, d + 1, edge].astype(jnp.float32)
            out[d, edge] = jnp.maximum(total, 0.0).astype(out.dtype)
            remote(ON_2, d).wait_recv()
            total = middle[d, core] + on_in[1, d] + field[c, d + 1, core].astype(jnp.float32)
            out[d, core] = jnp.maximum(total, 0.0).astype(out.dtype)

    own_copy.wait()
    for copy in filter_copies[: taps * taps]:
        copy.wait()
    repeat(depth + LAG, first_step)
    repeat(depth - EARLY, lambda d: remote(CORE, EARLY + d).start())
    for copy in filter_copies[taps * taps :]:
        copy.wait()
    pairs = depth // 2

    def drain_first(d):
        remote(VOLUME, d).wait_send()
        remote(ON_1, d).wait_send()

        @pl.when(has_off)
        def _():
            remote(OFF_1, d).wait_send()

    repeat(depth, drain_first)

    def drain_second(d):
        for kind in (EDGE, CORE):
            remote(kind, d).wait_send()

        @pl.when(has_off)
        def _():
            remote(OFF_2, d).wait_send()

    def second_step(i):
        is_core = jnp.logical_or(i == pairs - 1, i > pairs)
        at_core = jnp.where(i == pairs - 1, 0, i - pairs)

        @pl.when(jnp.logical_or(i < pairs - 1, i == pairs))
        def _():
            edge_step(jnp.minimum(i, pairs - 1))

        @pl.when(jnp.logical_and(is_core, i < 2 * pairs))
        def _():
            core_step(at_core)

        @pl.when(i == 2 * pairs)
        def _():
            repeat(depth, drain_second)

        @pl.when(i > pairs)
        def _():
            finish_pair(i - pairs - 1)

    repeat(2 * pairs + 1, second_step)
    repeat(depth, lambda d: remote(ON_2, d).wait_send())


def per_device(n_space, volume, first_filter, second_filter):
    depth, planes, width, half = volume.shape
    taps, _, _, in_c, out_c = first_filter.shape
    plane_buf = pltpu.VMEM((2, depth + 2, planes, width, half), jnp.bfloat16)
    filter_buf = pltpu.VMEM((taps, in_c, taps * taps * out_c), jnp.bfloat16)
    flops = 2 * 2 * 27 * depth * planes * width * in_c * out_c
    volume, first_filter, second_filter = (
        pltpu.with_memory_space_constraint(x, pltpu.HBM) for x in (volume, first_filter, second_filter)
    )
    return pl.pallas_call(
        functools.partial(kernel, n_space),
        out_shape=pltpu.VMEM(volume.shape, jnp.bfloat16),
        in_specs=[pl.BlockSpec(memory_space=pltpu.HBM)] * 3,
        out_specs=pl.BlockSpec(memory_space=pltpu.VMEM),
        scratch_shapes=[
            plane_buf,
            plane_buf,
            pltpu.VMEM((depth, planes, width, out_c), jnp.float32),
            pltpu.VMEM((2, depth, width, out_c), jnp.bfloat16),
            pltpu.VMEM((2, depth, width, out_c), jnp.bfloat16),
            pltpu.VMEM((2, depth, width, out_c), jnp.float32),
            pltpu.VMEM((2, depth, width, out_c), jnp.float32),
            filter_buf,
            filter_buf,
            pltpu.SemaphoreType.DMA((1 + 2 * taps * taps,)),
            pltpu.SemaphoreType.DMA((7, depth)),
            pltpu.SemaphoreType.DMA((7, depth)),
        ],
        compiler_params=pltpu.CompilerParams(
            collective_id=0, has_side_effects=True, vmem_limit_bytes=40 << 20
        ),
        cost_estimate=pl.CostEstimate(
            flops=flops, bytes_accessed=4 * volume.size + 4 * first_filter.size, transcendentals=0
        ),
    )(volume, first_filter, second_filter)


def solution(mesh):
    return jax.shard_map(
        functools.partial(per_device, mesh.shape["space"]),
        mesh=mesh,
        in_specs=(
            P(None, "space", None, "chan"),
            P(None, None, None, None, "chan"),
            P(None, None, None, None, "chan"),
        ),
        out_specs=P(None, "space", None, "chan"),
        check_vma=False,
    )
```

```python
import functools

import jax
import jax.numpy as jnp
from jax import lax
from jax.experimental import pallas as pl
from jax.experimental.pallas import tpu as pltpu
from jax.sharding import PartitionSpec as P

MESH = pl.DeviceIdType.MESH
LAG = 5
EARLY = 3
LATE = 2
EDGE, CORE = range(2)
VOLUME, OFF_1, ON_1, OFF_2, ON_2 = range(2, 7)
ON, OWN, OFF = range(3)


def shifted(left, middle, right):
    width = middle.shape[0]
    at = lax.broadcasted_iota(jnp.int32, middle.shape, 0)
    left = jnp.where(at == 0, 0.0, pltpu.roll(left, 1, 0))
    right = jnp.where(at == width - 1, 0.0, pltpu.roll(right, width - 1, 0))
    return left + middle + right


def repeat(count, body, first=0):
    def step(i, carry):
        body(i)
        return carry

    lax.fori_loop(first, count, step, 0)


def kernel(
    n_space, volume, first, second, out,
    field, hidden, middle, off_out, off_in, on_out, on_in, w1, w2, local_sem, send_sem, recv_sem,
):
    s, c = lax.axis_index("space"), lax.axis_index("chan")
    depth, planes, width, half = volume.shape
    taps, out_c = first.shape[0], first.shape[4]
    pairs = depth // 2
    odd = lax.rem(s, 2)
    has_off = jnp.where(odd == 0, s > 0, s < n_space - 1)
    on_dev, off_dev, across = {"space": s + 1 - 2 * odd}, {"space": s - 1 + 2 * odd}, {"chan": 1 - c}
    plane_at = (odd, 1 - odd)
    tap_of = (2 * odd, 1, 2 - 2 * odd)

    barrier = pltpu.get_barrier_semaphore()
    pl.semaphore_signal(barrier, inc=1, device_id=across, device_id_type=MESH)
    pl.semaphore_signal(barrier, inc=1, device_id=on_dev, device_id_type=MESH)

    @pl.when(has_off)
    def _():
        pl.semaphore_signal(barrier, inc=1, device_id=off_dev, device_id_type=MESH)

    own_copy = pltpu.make_async_copy(volume, field.at[c, pl.ds(1, depth)], local_sem.at[0])
    own_copy.start()
    filter_copies = []
    for k, (src, dst) in enumerate(((first, w1), (second, w2))):
        for role in range(3):
            for t in range(taps):
                col = role * taps + t
                filter_copies.append(
                    pltpu.make_async_copy(
                        src.at[:, tap_of[role], t],
                        dst.at[:, :, pl.ds(col * out_c, out_c)],
                        local_sem.at[1 + 3 * taps * k + col],
                    )
                )
    for copy in filter_copies:
        copy.start()

    rim = jnp.zeros((planes, width, half), field.dtype)
    for buf in (field, hidden):
        for h in range(2):
            buf[h, 0] = rim
            buf[h, depth + 1] = rim

    @pl.when(jnp.logical_not(has_off))
    def _():
        off_in[...] = jnp.zeros(off_in.shape, off_in.dtype)

    pl.semaphore_wait(barrier, 2 + has_off.astype(jnp.int32))

    def remote(kind, d):
        if kind == VOLUME:
            src, dst, dev = volume.at[d], field.at[c, d + 1], across
        elif kind in (EDGE, CORE):
            src = hidden.at[c, d + 1, plane_at[kind]]
            dst, dev = src, across
        elif kind in (OFF_1, OFF_2):
            k = 0 if kind == OFF_1 else 1
            src, dst, dev = off_out.at[k, d], off_in.at[k, d], off_dev
        else:
            k = 0 if kind == ON_1 else 1
            src, dst, dev = on_out.at[k, d], on_in.at[k, d], on_dev
        return pltpu.make_async_remote_copy(
            src_ref=src,
            dst_ref=dst,
            send_sem=send_sem.at[kind, d],
            recv_sem=recv_sem.at[kind, d],
            device_id=dev,
            device_id_type=MESH,
        )

    def start_off(kind, d):
        @pl.when(has_off)
        def _():
            remote(kind, d).start()

    def await_off(kind, d):
        @pl.when(has_off)
        def _():
            remote(kind, d).wait_recv()

    repeat(depth, lambda d: remote(VOLUME, d).start())

    def product(rows, w, roles):
        lhs = jnp.concatenate(rows, axis=1)
        per_role = taps * out_c
        cols = w[:, :, roles[0] * per_role : (roles[-1] + 1) * per_role]
        parts = jnp.dot(lhs, cols.reshape(lhs.shape[1], -1), preferred_element_type=jnp.float32)

        def combine(*terms):
            sums = []
            for t in range(taps):
                blocks = []
                for role, g in terms:
                    at = ((role - roles[0]) * taps + t) * out_c
                    blocks.append(parts[g * width : (g + 1) * width, at : at + out_c])
                sums.append(functools.reduce(jnp.add, blocks))
            return shifted(*sums)

        return combine

    def multiply_first(d):
        rows = [
            jnp.concatenate([field[h, d + a, plane_at[EDGE]], field[h, d + a, plane_at[CORE]]], axis=0)
            for a in range(taps)
            for h in range(2)
        ]
        combine = product(rows, w1, (ON, OWN, OFF))
        off_out[0, d] = combine((OFF, EDGE)).astype(off_out.dtype)
        start_off(OFF_1, d)
        on_out[0, d] = combine((ON, CORE))
        remote(ON_1, d).start()
        middle[d, EDGE] = combine((OWN, EDGE), (OFF, CORE))
        middle[d, CORE] = combine((OWN, CORE), (ON, EDGE))

    def finish_hidden(d):
        def store(kind, total):
            hidden[c, d + 1, plane_at[kind]] = jnp.maximum(total, 0.0).astype(hidden.dtype)

        await_off(OFF_1, d)
        store(EDGE, middle[d, EDGE] + off_in[0, d].astype(jnp.float32))
        remote(EDGE, d).start()
        remote(ON_1, d).wait_recv()
        store(CORE, middle[d, CORE] + on_in[0, d])

        @pl.when(d < EARLY)
        def _():
            remote(CORE, d).start()

    def first_step(t):
        @pl.when(t < depth)
        def _():
            remote(VOLUME, t).wait_recv()

        @pl.when(t >= LAG)
        def _():
            finish_hidden(t - LAG)

        @pl.when(jnp.logical_and(t >= 1, t <= depth))
        def _():
            multiply_first(t - 1)

    def plane_product(d, count, kind, roles):
        plane = plane_at[kind]
        rows = [
            jnp.concatenate([hidden[h, d + g + a, plane] for g in range(count)], axis=0)
            for a in range(taps)
            for h in range(2)
        ]
        return product(rows, w2, roles)

    def await_pair(kind, j):
        @pl.when(j == 0)
        def _():
            remote(kind, 0).wait_recv()

        remote(kind, 2 * j + 1).wait_recv()

        @pl.when(j < pairs - 1)
        def _():
            remote(kind, 2 * j + 2).wait_recv()

    def edge_step(j):
        await_pair(EDGE, j)
        combine = plane_product(2 * j, 2, EDGE, (ON, OWN, OFF))
        for g in range(2):
            off_out[1, 2 * j + g] = combine((OFF, g)).astype(off_out.dtype)
            start_off(OFF_2, 2 * j + g)
        for g in range(2):
            middle[2 * j + g, EDGE] = combine((OWN, g))
            middle[2 * j + g, CORE] = combine((ON, g))

    def core_sums(d, count, combine):
        for g in range(count):
            middle[d + g, CORE] = middle[d + g, CORE] + combine((OWN, g))
            middle[d + g, EDGE] = middle[d + g, EDGE] + combine((OFF, g))

    def core_send(d, count, combine):
        for g in range(count):
            on_out[1, d + g] = combine((ON, g))
            remote(ON_2, d + g).start()

    def core_step(j):
        await_pair(CORE, j)
        combine = plane_product(2 * j, 2, CORE, (ON, OWN, OFF))
        core_send(2 * j, 2, combine)
        core_sums(2 * j, 2, combine)

    def core_end(count):
        d = depth - count
        for k in range(d + 1, depth):
            remote(CORE, k).wait_recv()
        core_send(d, count, plane_product(d, count, CORE, (ON,)))

        @pl.when(s >= 0)
        def _():
            core_sums(d, count, plane_product(d, count, CORE, (OWN, OFF)))

    def finish_pair(j):
        def store(d, kind, other):
            plane = plane_at[kind]
            total = middle[d, kind] + other + field[c, d + 1, plane].astype(jnp.float32)
            out[d, plane] = jnp.maximum(total, 0.0).astype(out.dtype)

        for g in range(2):
            d = 2 * j + g
            await_off(OFF_2, d)
            store(d, EDGE, off_in[1, d].astype(jnp.float32))
        for g in range(2):
            d = 2 * j + g
            remote(ON_2, d).wait_recv()
            store(d, CORE, on_in[1, d])

    def drain(kinds, off_kind):
        def each(d):
            for kind in kinds:
                remote(kind, d).wait_send()

            @pl.when(has_off)
            def _():
                remote(off_kind, d).wait_send()

        repeat(depth, each)

    own_copy.wait()
    for copy in filter_copies[: 3 * taps]:
        copy.wait()
    repeat(depth + LAG, first_step)
    repeat(depth, lambda d: remote(CORE, d).start(), first=EARLY)
    for copy in filter_copies[3 * taps :]:
        copy.wait()
    drain((VOLUME, ON_1), OFF_1)

    whole = pairs - LATE

    def second_step(i):
        @pl.when(i != 1)
        def _():
            @pl.when(i <= pairs)
            def _():
                edge_step(jnp.maximum(i - 1, 0))

        @pl.when(jnp.logical_or(i == 1, i > pairs))
        def _():
            core_step(jnp.where(i == 1, 0, i - pairs))

    repeat(pairs + whole, second_step)
    repeat(whole, finish_pair)
    core_end(2 * LATE)
    drain((EDGE, CORE), OFF_2)
    repeat(pairs, finish_pair, first=whole)
    repeat(depth, lambda d: remote(ON_2, d).wait_send())


def per_device(n_space, volume, first_filter, second_filter):
    depth, planes, width, half = volume.shape
    taps, _, _, in_c, out_c = first_filter.shape
    plane_buf = pltpu.VMEM((2, depth + 2, planes, width, half), jnp.bfloat16)
    off_buf = pltpu.VMEM((2, depth, width, out_c), jnp.bfloat16)
    on_buf = pltpu.VMEM((2, depth, width, out_c), jnp.float32)
    filter_buf = pltpu.VMEM((taps, in_c, 3 * taps * out_c), jnp.bfloat16)
    flops = 2 * 2 * 27 * depth * planes * width * in_c * out_c
    volume, first_filter, second_filter = (
        pltpu.with_memory_space_constraint(x, pltpu.HBM) for x in (volume, first_filter, second_filter)
    )
    return pl.pallas_call(
        functools.partial(kernel, n_space),
        out_shape=pltpu.VMEM(volume.shape, jnp.bfloat16),
        in_specs=[pl.BlockSpec(memory_space=pltpu.HBM)] * 3,
        out_specs=pl.BlockSpec(memory_space=pltpu.VMEM),
        scratch_shapes=[
            plane_buf,
            plane_buf,
            pltpu.VMEM((depth, planes, width, out_c), jnp.float32),
            off_buf,
            off_buf,
            on_buf,
            on_buf,
            filter_buf,
            filter_buf,
            pltpu.SemaphoreType.DMA((1 + 6 * taps,)),
            pltpu.SemaphoreType.DMA((7, depth)),
            pltpu.SemaphoreType.DMA((7, depth)),
        ],
        compiler_params=pltpu.CompilerParams(
            collective_id=0, has_side_effects=True, vmem_limit_bytes=40 << 20
        ),
        cost_estimate=pl.CostEstimate(
            flops=flops, bytes_accessed=4 * volume.size + 4 * first_filter.size, transcendentals=0
        ),
    )(volume, first_filter, second_filter)


def solution(mesh):
    return jax.shard_map(
        functools.partial(per_device, mesh.shape["space"]),
        mesh=mesh,
        in_specs=(
            P(None, "space", None, "chan"),
            P(None, None, None, None, "chan"),
            P(None, None, None, None, "chan"),
        ),
        out_specs=P(None, "space", None, "chan"),
        check_vma=False,
    )
```

```python
import functools

import jax
import jax.numpy as jnp
from jax import lax
from jax.experimental import pallas as pl
from jax.experimental.pallas import tpu as pltpu
from jax.sharding import PartitionSpec as P

MESH = pl.DeviceIdType.MESH
LAG = 5
EARLY = 3
LATE = 2
EDGE, CORE = range(2)
VOLUME, OFF_1, ON_1, OFF_2, ON_2 = range(2, 7)
ON, OWN, OFF = range(3)


def shifted(left, middle, right):
    width = middle.shape[0]
    at = lax.broadcasted_iota(jnp.int32, middle.shape, 0)
    left = jnp.where(at == 0, 0.0, pltpu.roll(left, 1, 0))
    right = jnp.where(at == width - 1, 0.0, pltpu.roll(right, width - 1, 0))
    return left + middle + right


def repeat(count, body, first=0):
    def step(i, carry):
        body(i)
        return carry

    lax.fori_loop(first, count, step, 0)


def kernel(
    n_space, volume, first, second, out,
    field, hidden, middle, off_out, off_in, on_out, on_in, w1, w2, local_sem, send_sem, recv_sem,
):
    s, c = lax.axis_index("space"), lax.axis_index("chan")
    depth, planes, width, half = volume.shape
    taps, out_c = first.shape[0], first.shape[4]
    pairs = depth // 2
    odd = lax.rem(s, 2)
    has_off = jnp.where(odd == 0, s > 0, s < n_space - 1)
    on_dev, off_dev, across = {"space": s + 1 - 2 * odd}, {"space": s - 1 + 2 * odd}, {"chan": 1 - c}
    plane_at = (odd, 1 - odd)
    tap_of = (2 * odd, 1, 2 - 2 * odd)

    barrier = pltpu.get_barrier_semaphore()
    pl.semaphore_signal(barrier, inc=1, device_id=across, device_id_type=MESH)
    pl.semaphore_signal(barrier, inc=1, device_id=on_dev, device_id_type=MESH)

    @pl.when(has_off)
    def _():
        pl.semaphore_signal(barrier, inc=1, device_id=off_dev, device_id_type=MESH)

    own_copy = pltpu.make_async_copy(volume, field.at[c, pl.ds(1, depth)], local_sem.at[0])
    own_copy.start()
    for k, (src, dst) in enumerate(((first, w1), (second, w2))):
        for role in range(3):
            for t in range(taps):
                col = role * taps + t
                pltpu.make_async_copy(
                    src.at[:, tap_of[role], t],
                    dst.at[:, :, pl.ds(col * out_c, out_c)],
                    local_sem.at[1 + k],
                ).start()

    rim = jnp.zeros((planes, width, half), field.dtype)
    for buf in (field, hidden):
        for h in range(2):
            buf[h, 0] = rim
            buf[h, depth + 1] = rim

    @pl.when(jnp.logical_not(has_off))
    def _():
        off_in[...] = jnp.zeros(off_in.shape, off_in.dtype)

    pl.semaphore_wait(barrier, 2 + has_off.astype(jnp.int32))

    def remote(kind, d):
        if kind == VOLUME:
            src, dst, dev = volume.at[d], field.at[c, d + 1], across
        elif kind in (EDGE, CORE):
            src = hidden.at[c, d + 1, plane_at[kind]]
            dst, dev = src, across
        elif kind in (OFF_1, OFF_2):
            k = 0 if kind == OFF_1 else 1
            src, dst, dev = off_out.at[k, d], off_in.at[k, d], off_dev
        else:
            k = 0 if kind == ON_1 else 1
            src, dst, dev = on_out.at[k, d], on_in.at[k, d], on_dev
        return pltpu.make_async_remote_copy(
            src_ref=src,
            dst_ref=dst,
            send_sem=send_sem.at[kind],
            recv_sem=recv_sem.at[kind, d],
            device_id=dev,
            device_id_type=MESH,
        )

    def start_off(kind, d):
        @pl.when(has_off)
        def _():
            remote(kind, d).start()

    def await_off(kind, d):
        @pl.when(has_off)
        def _():
            remote(kind, d).wait_recv()

    repeat(depth, lambda d: remote(VOLUME, d).start())

    def product(rows, w, roles):
        lhs = jnp.concatenate(rows, axis=1)
        per_role = taps * out_c
        cols = w[:, :, roles[0] * per_role : (roles[-1] + 1) * per_role]
        parts = jnp.dot(lhs, cols.reshape(lhs.shape[1], -1), preferred_element_type=jnp.float32)

        def combine(*terms):
            sums = []
            for t in range(taps):
                blocks = []
                for role, g in terms:
                    at = ((role - roles[0]) * taps + t) * out_c
                    blocks.append(parts[g * width : (g + 1) * width, at : at + out_c])
                sums.append(functools.reduce(jnp.add, blocks))
            return shifted(*sums)

        return combine

    def multiply_first(d):
        rows = [
            jnp.concatenate([field[h, d + a, plane_at[EDGE]], field[h, d + a, plane_at[CORE]]], axis=0)
            for a in range(taps)
            for h in range(2)
        ]
        combine = product(rows, w1, (ON, OWN, OFF))
        off_out[0, d] = combine((OFF, EDGE)).astype(off_out.dtype)
        start_off(OFF_1, d)
        on_out[0, d] = combine((ON, CORE))
        remote(ON_1, d).start()
        middle[d, EDGE] = combine((OWN, EDGE), (OFF, CORE))
        middle[d, CORE] = combine((OWN, CORE), (ON, EDGE))

    def finish_hidden(d):
        def store(kind, total):
            hidden[c, d + 1, plane_at[kind]] = jnp.maximum(total, 0.0).astype(hidden.dtype)

        await_off(OFF_1, d)
        store(EDGE, middle[d, EDGE] + off_in[0, d].astype(jnp.float32))
        remote(EDGE, d).start()
        remote(ON_1, d).wait_recv()
        store(CORE, middle[d, CORE] + on_in[0, d])

        @pl.when(d < EARLY)
        def _():
            remote(CORE, d).start()

    def first_step(t):
        @pl.when(t < depth)
        def _():
            remote(VOLUME, t).wait_recv()

        @pl.when(t >= LAG)
        def _():
            finish_hidden(t - LAG)

        @pl.when(jnp.logical_and(t >= 1, t <= depth))
        def _():
            multiply_first(t - 1)

    def plane_product(d, count, kind, roles):
        plane = plane_at[kind]
        rows = [
            jnp.concatenate([hidden[h, d + g + a, plane] for g in range(count)], axis=0)
            for a in range(taps)
            for h in range(2)
        ]
        return product(rows, w2, roles)

    def await_pair(kind, j):
        @pl.when(j == 0)
        def _():
            remote(kind, 0).wait_recv()

        remote(kind, 2 * j + 1).wait_recv()

        @pl.when(j < pairs - 1)
        def _():
            remote(kind, 2 * j + 2).wait_recv()

    def edge_step(j):
        await_pair(EDGE, j)
        combine = plane_product(2 * j, 2, EDGE, (ON, OWN, OFF))
        for g in range(2):
            off_out[1, 2 * j + g] = combine((OFF, g)).astype(off_out.dtype)
            start_off(OFF_2, 2 * j + g)
        for g in range(2):
            middle[2 * j + g, EDGE] = combine((OWN, g))
            middle[2 * j + g, CORE] = combine((ON, g))

    def core_sums(d, count, combine):
        for g in range(count):
            middle[d + g, CORE] = middle[d + g, CORE] + combine((OWN, g))
            middle[d + g, EDGE] = middle[d + g, EDGE] + combine((OFF, g))

    def core_send(d, count, combine):
        for g in range(count):
            on_out[1, d + g] = combine((ON, g))
            remote(ON_2, d + g).start()

    def core_step(j):
        await_pair(CORE, j)
        combine = plane_product(2 * j, 2, CORE, (ON, OWN, OFF))
        core_send(2 * j, 2, combine)
        core_sums(2 * j, 2, combine)

    def core_end(count):
        d = depth - count
        for k in range(d + 1, depth):
            remote(CORE, k).wait_recv()
        core_send(d, count, plane_product(d, count, CORE, (ON,)))

        @pl.when(s >= 0)
        def _():
            core_sums(d, count, plane_product(d, count, CORE, (OWN, OFF)))

    def finish(kind, j):
        plane = plane_at[kind]
        for g in range(2):
            d = 2 * j + g
            if kind == EDGE:
                await_off(OFF_2, d)
                other = off_in[1, d].astype(jnp.float32)
            else:
                remote(ON_2, d).wait_recv()
                other = on_in[1, d]
            total = middle[d, kind] + other + field[c, d + 1, plane].astype(jnp.float32)
            out[d, plane] = jnp.maximum(total, 0.0).astype(out.dtype)

    def all_sent(kind):
        if kind == VOLUME:
            whole_ref = volume
        elif kind in (EDGE, CORE):
            whole_ref = hidden.at[c, pl.ds(1, depth), plane_at[kind]]
        else:
            whole_ref = (off_out if kind in (OFF_1, OFF_2) else on_out).at[0 if kind in (OFF_1, ON_1) else 1]
        pltpu.make_async_copy(whole_ref, whole_ref, send_sem.at[kind]).wait()

    def drain(kinds, off_kind=None):
        for kind in kinds:
            all_sent(kind)
        if off_kind is not None:
            @pl.when(has_off)
            def _():
                all_sent(off_kind)

    own_copy.wait()
    pltpu.make_async_copy(w1, w1, local_sem.at[1]).wait()
    repeat(depth + LAG, first_step)
    repeat(depth, lambda d: remote(CORE, d).start(), first=EARLY)
    pltpu.make_async_copy(w2, w2, local_sem.at[2]).wait()
    drain((VOLUME, ON_1), OFF_1)

    whole = pairs - LATE

    def second_step(i):
        @pl.when(i != 1)
        def _():
            @pl.when(i <= pairs)
            def _():
                edge_step(jnp.maximum(i - 1, 0))

        @pl.when(jnp.logical_or(i == 1, i > pairs))
        def _():
            core_step(jnp.where(i == 1, 0, i - pairs))

    repeat(pairs + whole, second_step)
    for kind in (EDGE, CORE):
        repeat(whole, lambda j: finish(kind, j))
    core_end(2 * LATE)
    repeat(pairs, lambda j: finish(EDGE, j), first=whole)
    drain((EDGE, CORE), OFF_2)
    repeat(pairs, lambda j: finish(CORE, j), first=whole)
    drain((ON_2,))


def per_device(n_space, volume, first_filter, second_filter):
    depth, planes, width, half = volume.shape
    taps, _, _, in_c, out_c = first_filter.shape
    plane_buf = pltpu.VMEM((2, depth + 2, planes, width, half), jnp.bfloat16)
    off_buf = pltpu.VMEM((2, depth, width, out_c), jnp.bfloat16)
    on_buf = pltpu.VMEM((2, depth, width, out_c), jnp.float32)
    filter_buf = pltpu.VMEM((taps, in_c, 3 * taps * out_c), jnp.bfloat16)
    flops = 2 * 2 * 27 * depth * planes * width * in_c * out_c
    volume, first_filter, second_filter = (
        pltpu.with_memory_space_constraint(x, pltpu.HBM) for x in (volume, first_filter, second_filter)
    )
    return pl.pallas_call(
        functools.partial(kernel, n_space),
        out_shape=pltpu.VMEM(volume.shape, jnp.bfloat16),
        in_specs=[pl.BlockSpec(memory_space=pltpu.HBM)] * 3,
        out_specs=pl.BlockSpec(memory_space=pltpu.VMEM),
        scratch_shapes=[
            plane_buf,
            plane_buf,
            pltpu.VMEM((depth, planes, width, out_c), jnp.float32),
            off_buf,
            off_buf,
            on_buf,
            on_buf,
            filter_buf,
            filter_buf,
            pltpu.SemaphoreType.DMA((3,)),
            pltpu.SemaphoreType.DMA((7,)),
            pltpu.SemaphoreType.DMA((7, depth)),
        ],
        compiler_params=pltpu.CompilerParams(
            collective_id=0, has_side_effects=True, vmem_limit_bytes=40 << 20
        ),
        cost_estimate=pl.CostEstimate(
            flops=flops, bytes_accessed=4 * volume.size + 4 * first_filter.size, transcendentals=0
        ),
    )(volume, first_filter, second_filter)


def solution(mesh):
    return jax.shard_map(
        functools.partial(per_device, mesh.shape["space"]),
        mesh=mesh,
        in_specs=(
            P(None, "space", None, "chan"),
            P(None, None, None, None, "chan"),
            P(None, None, None, None, "chan"),
        ),
        out_specs=P(None, "space", None, "chan"),
        check_vma=False,
    )
```

```python
import functools

import jax
import jax.numpy as jnp
from jax import lax
from jax.experimental import pallas as pl
from jax.experimental.pallas import tpu as pltpu
from jax.sharding import PartitionSpec as P

MESH = pl.DeviceIdType.MESH
LATE = 2
EARLY = 1
EDGE, CORE, TO_OFF, TO_ON = range(4)
ON, OWN, OFF = range(3)


def shifted(left, middle, right):
    width = middle.shape[0]
    at = lax.broadcasted_iota(jnp.int32, middle.shape, 0)
    left = jnp.where(at == 0, 0.0, pltpu.roll(left, 1, 0))
    right = jnp.where(at == width - 1, 0.0, pltpu.roll(right, width - 1, 0))
    return left + middle + right


def repeat(count, body, first=0):
    def step(i, carry):
        body(i)
        return carry

    lax.fori_loop(first, count, step, 0)


def kernel(
    n_space, volume, first, second, out,
    field, hidden, middle, off_out, off_in, on_out, on_in, w1, w2, local_sem, send_sem, recv_sem,
):
    s, c = lax.axis_index("space"), lax.axis_index("chan")
    depth, planes, width, half = volume.shape
    taps, out_c = first.shape[0], first.shape[4]
    pairs = depth // 2
    odd = lax.rem(s, 2)
    has_off = jnp.where(odd == 0, s > 0, s < n_space - 1)
    on_dev, off_dev, across = {"space": s + 1 - 2 * odd}, {"space": s - 1 + 2 * odd}, {"chan": 1 - c}
    plane_at = (odd, 1 - odd)
    tap_of = (2 * odd, 1, 2 - 2 * odd)

    barrier = pltpu.get_barrier_semaphore()
    pl.semaphore_signal(barrier, inc=1, device_id=across, device_id_type=MESH)
    pl.semaphore_signal(barrier, inc=1, device_id=on_dev, device_id_type=MESH)

    @pl.when(has_off)
    def _():
        pl.semaphore_signal(barrier, inc=1, device_id=off_dev, device_id_type=MESH)

    own_copy = pltpu.make_async_copy(volume, field.at[c, pl.ds(1, depth)], local_sem.at[0])
    own_copy.start()
    for k, (src, dst) in enumerate(((first, w1), (second, w2))):
        for role in range(3):
            for t in range(taps):
                col = role * taps + t
                pltpu.make_async_copy(
                    src.at[:, tap_of[role], t],
                    dst.at[:, :, pl.ds(col * out_c, out_c)],
                    local_sem.at[1 + k],
                ).start()

    rim = jnp.zeros((planes, width, half), field.dtype)
    for buf in (field, hidden):
        for h in range(2):
            buf[h, 0] = rim
            buf[h, depth + 1] = rim

    @pl.when(jnp.logical_not(has_off))
    def _():
        off_in[...] = jnp.zeros(off_in.shape, off_in.dtype)

    pl.semaphore_wait(barrier, 2 + has_off.astype(jnp.int32))

    def remote(k, kind, d):
        if kind in (EDGE, CORE):
            plane = plane_at[kind]
            dst, dev = (field, hidden)[k].at[c, d + 1, plane], across
            src = volume.at[d, plane] if k == 0 else dst
        elif kind == TO_OFF:
            src, dst, dev = off_out.at[k, d], off_in.at[k, d], off_dev
        else:
            src, dst, dev = on_out.at[k, d], on_in.at[k, d], on_dev
        return pltpu.make_async_remote_copy(
            src_ref=src,
            dst_ref=dst,
            send_sem=send_sem.at[k, kind],
            recv_sem=recv_sem.at[k, kind, d],
            device_id=dev,
            device_id_type=MESH,
        )

    head = pairs // 2
    repeat(2 * head + 1, lambda d: remote(0, EDGE, d).start())
    repeat(2 * head - 1, lambda d: remote(0, CORE, d).start())
    remote(0, EDGE, 2 * head + 1).start()
    repeat(2 * head + 1, lambda d: remote(0, CORE, d).start(), first=2 * head - 1)
    repeat(depth, lambda d: remote(0, EDGE, d).start(), first=2 * head + 2)
    repeat(depth, lambda d: remote(0, CORE, d).start(), first=2 * head + 1)

    def product(rows, w, roles):
        lhs = jnp.concatenate(rows, axis=1)
        per_role = taps * out_c
        cols = w[:, :, roles[0] * per_role : (roles[-1] + 1) * per_role]
        parts = jnp.dot(lhs, cols.reshape(lhs.shape[1], -1), preferred_element_type=jnp.float32)

        def combine(*terms):
            sums = []
            for t in range(taps):
                blocks = []
                for role, g in terms:
                    at = ((role - roles[0]) * taps + t) * out_c
                    blocks.append(parts[g * width : (g + 1) * width, at : at + out_c])
                sums.append(functools.reduce(jnp.add, blocks))
            return shifted(*sums)

        return combine

    def plane_product(k, kind, d, count, roles):
        buf, plane = (field, hidden)[k], plane_at[kind]
        rows = [
            jnp.concatenate([buf[h, d + g + a, plane] for g in range(count)], axis=0)
            for a in range(taps)
            for h in range(2)
        ]
        return product(rows, (w1, w2)[k], roles)

    def await_pair(k, kind, j):
        @pl.when(j == 0)
        def _():
            remote(k, kind, 0).wait_recv()

        remote(k, kind, 2 * j + 1).wait_recv()

        @pl.when(j < pairs - 1)
        def _():
            remote(k, kind, 2 * j + 2).wait_recv()

    def edge_step(k, j):
        await_pair(k, EDGE, j)
        combine = plane_product(k, EDGE, 2 * j, 2, (ON, OWN, OFF))
        for g in range(2):
            d = 2 * j + g
            off_out[k, d] = combine((OFF, g)).astype(off_out.dtype)

            @pl.when(has_off)
            def _():
                remote(k, TO_OFF, d).start()

        for g in range(2):
            middle[2 * j + g, EDGE] = combine((OWN, g))
            middle[2 * j + g, CORE] = combine((ON, g))

    def core_sums(d, count, combine):
        for g in range(count):
            middle[d + g, EDGE] = middle[d + g, EDGE] + combine((OFF, g))
            middle[d + g, CORE] = middle[d + g, CORE] + combine((OWN, g))

    def core_send(k, d, count, combine):
        for g in range(count):
            on_out[k, d + g] = combine((ON, g))
            remote(k, TO_ON, d + g).start()

    def core_step(k, j):
        await_pair(k, CORE, j)
        combine = plane_product(k, CORE, 2 * j, 2, (ON, OWN, OFF))
        core_send(k, 2 * j, 2, combine)
        core_sums(2 * j, 2, combine)

    def core_end(k, count):
        d = depth - count
        for at in range(d + 1, depth):
            remote(k, CORE, at).wait_recv()
        core_send(k, d, count, plane_product(k, CORE, d, count, (ON,)))

        @pl.when(s >= 0)
        def _():
            core_sums(d, count, plane_product(k, CORE, d, count, (OWN, OFF)))

    def store(k, kind, d, other):
        plane = plane_at[kind]
        total = middle[d, kind] + other
        if k == 0:
            hidden[c, d + 1, plane] = jnp.maximum(total, 0.0).astype(hidden.dtype)
        else:
            total = total + field[c, d + 1, plane].astype(jnp.float32)
            out[d, plane] = jnp.maximum(total, 0.0).astype(out.dtype)

    def finish_edge(k, j):
        for g in range(2):
            d = 2 * j + g

            @pl.when(has_off)
            def _():
                remote(k, TO_OFF, d).wait_recv()

            store(k, EDGE, d, off_in[k, d].astype(jnp.float32))
            if k == 0:
                remote(1, EDGE, d).start()

    def finish_core(k, j):
        for g in range(2):
            d = 2 * j + g
            remote(k, TO_ON, d).wait_recv()
            store(k, CORE, d, on_in[k, d])

    def all_sent(k, kind):
        if kind in (EDGE, CORE):
            whole_ref = (field, hidden)[k].at[c, pl.ds(1, depth), plane_at[kind]]
        else:
            whole_ref = (off_out if kind == TO_OFF else on_out).at[k]
        pltpu.make_async_copy(whole_ref, whole_ref, send_sem.at[k, kind]).wait()

    def drain(k, kinds):
        for kind in kinds:
            if kind == TO_OFF:
                @pl.when(has_off)
                def _():
                    all_sent(k, TO_OFF)
            else:
                all_sent(k, kind)

    own_copy.wait()
    pltpu.make_async_copy(w1, w1, local_sem.at[1]).wait()
    def hidden_step(i):
        is_edge = jnp.logical_or(i < head, jnp.logical_and(i >= 2 * head, i < pairs + head))
        at = jnp.where(i < 2 * head, i - head, i - pairs)

        @pl.when(is_edge)
        def _():
            edge_step(0, jnp.where(i < head, i, i - head))

        @pl.when(jnp.logical_and(jnp.logical_not(is_edge), i < 2 * pairs))
        def _():
            core_step(0, at)
            finish_edge(0, at)

        @pl.when(jnp.logical_and(jnp.logical_not(is_edge), i != head))
        def _():
            finish_core(0, at - 1)

            @pl.when(at - 1 < EARLY)
            def _():
                for g in range(2):
                    remote(1, CORE, 2 * (at - 1) + g).start()

    repeat(2 * pairs + 1, hidden_step)
    repeat(depth, lambda d: remote(1, CORE, d).start(), first=2 * EARLY)
    pltpu.make_async_copy(w2, w2, local_sem.at[2]).wait()
    drain(0, (EDGE, CORE, TO_OFF, TO_ON))

    repeat(pairs, lambda j: edge_step(1, j))
    whole = pairs - LATE
    repeat(whole, lambda j: core_step(1, j))

    def finish(j):
        finish_edge(1, j)
        finish_core(1, j)

    repeat(whole, finish)
    core_end(1, 2 * LATE)
    repeat(pairs, lambda j: finish_edge(1, j), first=whole)
    drain(1, (EDGE, CORE, TO_OFF))
    repeat(pairs, lambda j: finish_core(1, j), first=whole)
    drain(1, (TO_ON,))


def per_device(n_space, volume, first_filter, second_filter):
    depth, planes, width, half = volume.shape
    taps, _, _, in_c, out_c = first_filter.shape
    plane_buf = pltpu.VMEM((2, depth + 2, planes, width, half), jnp.bfloat16)
    off_buf = pltpu.VMEM((2, depth, width, out_c), jnp.bfloat16)
    on_buf = pltpu.VMEM((2, depth, width, out_c), jnp.float32)
    filter_buf = pltpu.VMEM((taps, in_c, 3 * taps * out_c), jnp.bfloat16)
    flops = 2 * 2 * 27 * depth * planes * width * in_c * out_c
    volume, first_filter, second_filter = (
        pltpu.with_memory_space_constraint(x, pltpu.HBM) for x in (volume, first_filter, second_filter)
    )
    return pl.pallas_call(
        functools.partial(kernel, n_space),
        out_shape=pltpu.VMEM(volume.shape, jnp.bfloat16),
        in_specs=[pl.BlockSpec(memory_space=pltpu.HBM)] * 3,
        out_specs=pl.BlockSpec(memory_space=pltpu.VMEM),
        scratch_shapes=[
            plane_buf,
            plane_buf,
            pltpu.VMEM((depth, planes, width, out_c), jnp.float32),
            off_buf,
            off_buf,
            on_buf,
            on_buf,
            filter_buf,
            filter_buf,
            pltpu.SemaphoreType.DMA((3,)),
            pltpu.SemaphoreType.DMA((2, 4)),
            pltpu.SemaphoreType.DMA((2, 4, depth)),
        ],
        compiler_params=pltpu.CompilerParams(
            collective_id=0, has_side_effects=True, vmem_limit_bytes=40 << 20
        ),
        cost_estimate=pl.CostEstimate(
            flops=flops, bytes_accessed=4 * volume.size + 4 * first_filter.size, transcendentals=0
        ),
    )(volume, first_filter, second_filter)


def solution(mesh):
    return jax.shard_map(
        functools.partial(per_device, mesh.shape["space"]),
        mesh=mesh,
        in_specs=(
            P(None, "space", None, "chan"),
            P(None, None, None, None, "chan"),
            P(None, None, None, None, "chan"),
        ),
        out_specs=P(None, "space", None, "chan"),
        check_vma=False,
    )
```

```python
import functools

import jax
import jax.numpy as jnp
from jax import lax
from jax.experimental import pallas as pl
from jax.experimental.pallas import tpu as pltpu
from jax.sharding import PartitionSpec as P

MESH = pl.DeviceIdType.MESH
LAG = 5
EARLY = 3
LATE = 2
EDGE, CORE = range(2)
VOLUME, OFF_1, ON_1, OFF_2, ON_2 = range(2, 7)
ON, OWN, OFF = range(3)


def shifted(left, middle, right):
    width = middle.shape[0]
    at = lax.broadcasted_iota(jnp.int32, middle.shape, 0)
    left = jnp.where(at == 0, 0.0, pltpu.roll(left, 1, 0))
    right = jnp.where(at == width - 1, 0.0, pltpu.roll(right, width - 1, 0))
    return left + middle + right


def repeat(count, body, first=0):
    def step(i, carry):
        body(i)
        return carry

    lax.fori_loop(first, count, step, 0)


def kernel(
    n_space, volume, first, second, out,
    field, hidden, middle, off_out, off_in, on_out, on_in, w1, w2, local_sem, send_sem, recv_sem,
):
    s, c = lax.axis_index("space"), lax.axis_index("chan")
    depth, planes, width, half = volume.shape
    taps, out_c = first.shape[0], first.shape[4]
    pairs = depth // 2
    odd = lax.rem(s, 2)
    has_off = jnp.where(odd == 0, s > 0, s < n_space - 1)
    on_dev, off_dev, across = {"space": s + 1 - 2 * odd}, {"space": s - 1 + 2 * odd}, {"chan": 1 - c}
    plane_at = (odd, 1 - odd)
    tap_of = (2 * odd, 1, 2 - 2 * odd)

    barrier = pltpu.get_barrier_semaphore()
    pl.semaphore_signal(barrier, inc=1, device_id=across, device_id_type=MESH)
    pl.semaphore_signal(barrier, inc=1, device_id=on_dev, device_id_type=MESH)

    @pl.when(has_off)
    def _():
        pl.semaphore_signal(barrier, inc=1, device_id=off_dev, device_id_type=MESH)

    own_copy = pltpu.make_async_copy(volume, field.at[c, pl.ds(1, depth)], local_sem.at[0])
    own_copy.start()
    for k, (src, dst) in enumerate(((first, w1), (second, w2))):
        for role in range(3):
            for t in range(taps):
                col = role * taps + t
                pltpu.make_async_copy(
                    src.at[:, tap_of[role], t],
                    dst.at[:, :, pl.ds(col * out_c, out_c)],
                    local_sem.at[1 + k],
                ).start()

    rim = jnp.zeros((planes, width, half), field.dtype)
    for buf in (field, hidden):
        for h in range(2):
            buf[h, 0] = rim
            buf[h, depth + 1] = rim

    @pl.when(jnp.logical_not(has_off))
    def _():
        off_in[...] = jnp.zeros(off_in.shape, off_in.dtype)

    pl.semaphore_wait(barrier, 2 + has_off.astype(jnp.int32))

    def remote(kind, d, count=1):
        if kind == VOLUME:
            src, dst, dev = volume.at[d], field.at[c, d + 1], across
        elif kind in (EDGE, CORE):
            src = hidden.at[c, pl.ds(d + 1, count), plane_at[kind]]
            dst, dev = src, across
        elif kind in (OFF_1, OFF_2):
            k = 0 if kind == OFF_1 else 1
            src, dst, dev = off_out.at[k, d], off_in.at[k, d], off_dev
        else:
            k = 0 if kind == ON_1 else 1
            src, dst, dev = on_out.at[k, d], on_in.at[k, d], on_dev
        return pltpu.make_async_remote_copy(
            src_ref=src,
            dst_ref=dst,
            send_sem=send_sem.at[kind],
            recv_sem=recv_sem.at[kind, d],
            device_id=dev,
            device_id_type=MESH,
        )

    def start_off(kind, d):
        @pl.when(has_off)
        def _():
            remote(kind, d).start()

    def await_off(kind, d):
        @pl.when(has_off)
        def _():
            remote(kind, d).wait_recv()

    repeat(depth, lambda d: remote(VOLUME, d).start())

    def product(rows, w, roles):
        lhs = jnp.concatenate(rows, axis=1)
        per_role = taps * out_c
        cols = w[:, :, roles[0] * per_role : (roles[-1] + 1) * per_role]
        parts = jnp.dot(lhs, cols.reshape(lhs.shape[1], -1), preferred_element_type=jnp.float32)

        def combine(*terms):
            sums = []
            for t in range(taps):
                blocks = []
                for role, g in terms:
                    at = ((role - roles[0]) * taps + t) * out_c
                    blocks.append(parts[g * width : (g + 1) * width, at : at + out_c])
                sums.append(functools.reduce(jnp.add, blocks))
            return shifted(*sums)

        return combine

    def multiply_first(d):
        rows = [
            jnp.concatenate([field[h, d + a, plane_at[EDGE]], field[h, d + a, plane_at[CORE]]], axis=0)
            for a in range(taps)
            for h in range(2)
        ]
        combine = product(rows, w1, (ON, OWN, OFF))
        off_out[0, d] = combine((OFF, EDGE)).astype(off_out.dtype)
        start_off(OFF_1, d)
        on_out[0, d] = combine((ON, CORE))
        remote(ON_1, d).start()
        middle[d, EDGE] = combine((OWN, EDGE), (OFF, CORE))
        middle[d, CORE] = combine((OWN, CORE), (ON, EDGE))

    def finish_hidden(d):
        def store(kind, total):
            hidden[c, d + 1, plane_at[kind]] = jnp.maximum(total, 0.0).astype(hidden.dtype)

        await_off(OFF_1, d)
        store(EDGE, middle[d, EDGE] + off_in[0, d].astype(jnp.float32))
        remote(EDGE, d).start()
        remote(ON_1, d).wait_recv()
        store(CORE, middle[d, CORE] + on_in[0, d])

        @pl.when(d < EARLY)
        def _():
            remote(CORE, d).start()

    def first_step(t):
        @pl.when(t < depth)
        def _():
            remote(VOLUME, t).wait_recv()

        @pl.when(t >= LAG)
        def _():
            finish_hidden(t - LAG)

        @pl.when(jnp.logical_and(t >= 1, t <= depth))
        def _():
            multiply_first(t - 1)

    def plane_product(d, count, kind, roles):
        plane = plane_at[kind]
        rows = [
            jnp.concatenate([hidden[h, d + g + a, plane] for g in range(count)], axis=0)
            for a in range(taps)
            for h in range(2)
        ]
        return product(rows, w2, roles)

    def await_pair(kind, j):
        @pl.when(j == 0)
        def _():
            remote(kind, 0).wait_recv()

        remote(kind, 2 * j + 1).wait_recv()

        @pl.when(j < pairs - 1)
        def _():
            remote(kind, 2 * j + 2).wait_recv()

    def await_core(j):
        @pl.when(j == 0)
        def _():
            for d in range(EARLY):
                remote(CORE, d).wait_recv()

        @pl.when(jnp.logical_and(j > 0, j < pairs - 1))
        def _():
            remote(CORE, 2 * j + 1, 2).wait_recv()

        @pl.when(j == pairs - 1)
        def _():
            remote(CORE, depth - 1).wait_recv()

    def edge_step(j):
        await_pair(EDGE, j)
        combine = plane_product(2 * j, 2, EDGE, (ON, OWN, OFF))
        for g in range(2):
            off_out[1, 2 * j + g] = combine((OFF, g)).astype(off_out.dtype)
            start_off(OFF_2, 2 * j + g)
        for g in range(2):
            middle[2 * j + g, EDGE] = combine((OWN, g))
            middle[2 * j + g, CORE] = combine((ON, g))

    def core_sums(d, count, combine):
        for g in range(count):
            middle[d + g, CORE] = middle[d + g, CORE] + combine((OWN, g))
            middle[d + g, EDGE] = middle[d + g, EDGE] + combine((OFF, g))

    def core_send(d, count, combine):
        for g in range(count):
            on_out[1, d + g] = combine((ON, g))
            remote(ON_2, d + g).start()

    def core_step(j):
        await_core(j)
        combine = plane_product(2 * j, 2, CORE, (ON, OWN, OFF))
        core_send(2 * j, 2, combine)
        core_sums(2 * j, 2, combine)

    def core_end(count):
        d = depth - count
        for j in range(d // 2, pairs):
            await_core(jnp.int32(j))
        core_send(d, count, plane_product(d, count, CORE, (ON,)))

        @pl.when(s >= 0)
        def _():
            core_sums(d, count, plane_product(d, count, CORE, (OWN, OFF)))

    def finish(kind, j):
        plane = plane_at[kind]
        for g in range(2):
            d = 2 * j + g
            if kind == EDGE:
                await_off(OFF_2, d)
                other = off_in[1, d].astype(jnp.float32)
            else:
                remote(ON_2, d).wait_recv()
                other = on_in[1, d]
            total = middle[d, kind] + other + field[c, d + 1, plane].astype(jnp.float32)
            out[d, plane] = jnp.maximum(total, 0.0).astype(out.dtype)

    def all_sent(kind):
        if kind == VOLUME:
            whole_ref = volume
        elif kind in (EDGE, CORE):
            whole_ref = hidden.at[c, pl.ds(1, depth), plane_at[kind]]
        else:
            whole_ref = (off_out if kind in (OFF_1, OFF_2) else on_out).at[0 if kind in (OFF_1, ON_1) else 1]
        pltpu.make_async_copy(whole_ref, whole_ref, send_sem.at[kind]).wait()

    def drain(kinds, off_kind=None):
        for kind in kinds:
            all_sent(kind)
        if off_kind is not None:
            @pl.when(has_off)
            def _():
                all_sent(off_kind)

    own_copy.wait()
    pltpu.make_async_copy(w1, w1, local_sem.at[1]).wait()
    repeat(depth + LAG, first_step)
    repeat(pairs - 1, lambda j: remote(CORE, 2 * j + 1, 2).start(), first=1)
    remote(CORE, depth - 1).start()
    pltpu.make_async_copy(w2, w2, local_sem.at[2]).wait()
    drain((VOLUME, ON_1), OFF_1)

    whole = pairs - LATE

    def second_step(i):
        @pl.when(i != 1)
        def _():
            @pl.when(i <= pairs)
            def _():
                edge_step(jnp.maximum(i - 1, 0))

        @pl.when(jnp.logical_or(i == 1, i > pairs))
        def _():
            core_step(jnp.where(i == 1, 0, i - pairs))

    repeat(pairs + whole, second_step)
    for kind in (EDGE, CORE):
        repeat(whole, lambda j: finish(kind, j))
    core_end(2 * LATE)
    repeat(pairs, lambda j: finish(EDGE, j), first=whole)
    drain((EDGE, CORE), OFF_2)
    repeat(pairs, lambda j: finish(CORE, j), first=whole)
    drain((ON_2,))


def per_device(n_space, volume, first_filter, second_filter):
    depth, planes, width, half = volume.shape
    taps, _, _, in_c, out_c = first_filter.shape
    plane_buf = pltpu.VMEM((2, depth + 2, planes, width, half), jnp.bfloat16)
    off_buf = pltpu.VMEM((2, depth, width, out_c), jnp.bfloat16)
    on_buf = pltpu.VMEM((2, depth, width, out_c), jnp.float32)
    filter_buf = pltpu.VMEM((taps, in_c, 3 * taps * out_c), jnp.bfloat16)
    flops = 2 * 2 * 27 * depth * planes * width * in_c * out_c
    volume, first_filter, second_filter = (
        pltpu.with_memory_space_constraint(x, pltpu.HBM) for x in (volume, first_filter, second_filter)
    )
    return pl.pallas_call(
        functools.partial(kernel, n_space),
        out_shape=pltpu.VMEM(volume.shape, jnp.bfloat16),
        in_specs=[pl.BlockSpec(memory_space=pltpu.HBM)] * 3,
        out_specs=pl.BlockSpec(memory_space=pltpu.VMEM),
        scratch_shapes=[
            plane_buf,
            plane_buf,
            pltpu.VMEM((depth, planes, width, out_c), jnp.float32),
            off_buf,
            off_buf,
            on_buf,
            on_buf,
            filter_buf,
            filter_buf,
            pltpu.SemaphoreType.DMA((3,)),
            pltpu.SemaphoreType.DMA((7,)),
            pltpu.SemaphoreType.DMA((7, depth)),
        ],
        compiler_params=pltpu.CompilerParams(
            collective_id=0, has_side_effects=True, vmem_limit_bytes=40 << 20
        ),
        cost_estimate=pl.CostEstimate(
            flops=flops, bytes_accessed=4 * volume.size + 4 * first_filter.size, transcendentals=0
        ),
    )(volume, first_filter, second_filter)


def solution(mesh):
    return jax.shard_map(
        functools.partial(per_device, mesh.shape["space"]),
        mesh=mesh,
        in_specs=(
            P(None, "space", None, "chan"),
            P(None, None, None, None, "chan"),
            P(None, None, None, None, "chan"),
        ),
        out_specs=P(None, "space", None, "chan"),
        check_vma=False,
    )
```

```python
import functools

import jax
import jax.numpy as jnp
from jax import lax
from jax.experimental import pallas as pl
from jax.experimental.pallas import tpu as pltpu
from jax.sharding import PartitionSpec as P

MESH = pl.DeviceIdType.MESH
LAG = 4
EARLY = 3
LATE = 2
EDGE, CORE = range(2)
VOLUME, OFF_1, ON_1, OFF_2, ON_2 = range(2, 7)
ON, OWN, OFF = range(3)


def shifted(left, middle, right):
    width = middle.shape[0]
    at = lax.broadcasted_iota(jnp.int32, middle.shape, 0)
    left = jnp.where(at == 0, 0.0, pltpu.roll(left, 1, 0))
    right = jnp.where(at == width - 1, 0.0, pltpu.roll(right, width - 1, 0))
    return left + middle + right


def repeat(count, body, first=0):
    def step(i, carry):
        body(i)
        return carry

    lax.fori_loop(first, count, step, 0)


def kernel(
    n_space, volume, first, second, out,
    field, hidden, middle, off_out, off_in, on_out, on_in, w1, w2, local_sem, send_sem, recv_sem,
):
    s, c = lax.axis_index("space"), lax.axis_index("chan")
    depth, planes, width, half = volume.shape
    taps, out_c = first.shape[0], first.shape[4]
    pairs = depth // 2
    odd = lax.rem(s, 2)
    has_off = jnp.where(odd == 0, s > 0, s < n_space - 1)
    on_dev, off_dev, across = {"space": s + 1 - 2 * odd}, {"space": s - 1 + 2 * odd}, {"chan": 1 - c}
    plane_at = (odd, 1 - odd)
    tap_of = (2 * odd, 1, 2 - 2 * odd)

    barrier = pltpu.get_barrier_semaphore()
    pl.semaphore_signal(barrier, inc=1, device_id=across, device_id_type=MESH)
    pl.semaphore_signal(barrier, inc=1, device_id=on_dev, device_id_type=MESH)

    @pl.when(has_off)
    def _():
        pl.semaphore_signal(barrier, inc=1, device_id=off_dev, device_id_type=MESH)

    own_copy = pltpu.make_async_copy(volume, field.at[c, pl.ds(1, depth)], local_sem.at[0])
    own_copy.start()
    for k, (src, dst) in enumerate(((first, w1), (second, w2))):
        for role in range(3):
            for t in range(taps):
                col = role * taps + t
                pltpu.make_async_copy(
                    src.at[:, tap_of[role], t],
                    dst.at[:, :, pl.ds(col * out_c, out_c)],
                    local_sem.at[1 + k],
                ).start()

    rim = jnp.zeros((planes, width, half), field.dtype)
    for buf in (field, hidden):
        for h in range(2):
            buf[h, 0] = rim
            buf[h, depth + 1] = rim

    @pl.when(jnp.logical_not(has_off))
    def _():
        off_in[...] = jnp.zeros(off_in.shape, off_in.dtype)

    pl.semaphore_wait(barrier, 2 + has_off.astype(jnp.int32))

    def remote(kind, d, count=1):
        if kind == VOLUME:
            src, dst, dev = volume.at[d], field.at[c, d + 1], across
        elif kind in (EDGE, CORE):
            src = hidden.at[c, pl.ds(d + 1, count), plane_at[kind]]
            dst, dev = src, across
        elif kind in (OFF_1, OFF_2):
            k = 0 if kind == OFF_1 else 1
            src, dst, dev = off_out.at[k, d], off_in.at[k, d], off_dev
        else:
            k = 0 if kind == ON_1 else 1
            src, dst, dev = on_out.at[k, d], on_in.at[k, d], on_dev
        return pltpu.make_async_remote_copy(
            src_ref=src,
            dst_ref=dst,
            send_sem=send_sem.at[kind],
            recv_sem=recv_sem.at[kind, d],
            device_id=dev,
            device_id_type=MESH,
        )

    def start_off(kind, d):
        @pl.when(has_off)
        def _():
            remote(kind, d).start()

    def await_off(kind, d):
        @pl.when(has_off)
        def _():
            remote(kind, d).wait_recv()

    repeat(depth, lambda d: remote(VOLUME, d).start())

    def product(rows, w, roles):
        lhs = jnp.concatenate(rows, axis=1)
        per_role = taps * out_c
        cols = w[:, :, roles[0] * per_role : (roles[-1] + 1) * per_role]
        parts = jnp.dot(lhs, cols.reshape(lhs.shape[1], -1), preferred_element_type=jnp.float32)

        def combine(*terms):
            sums = []
            for t in range(taps):
                blocks = []
                for role, g in terms:
                    at = ((role - roles[0]) * taps + t) * out_c
                    blocks.append(parts[g * width : (g + 1) * width, at : at + out_c])
                sums.append(functools.reduce(jnp.add, blocks))
            return shifted(*sums)

        return combine

    def multiply_first(d):
        rows = [
            jnp.concatenate([field[h, d + a, plane_at[EDGE]], field[h, d + a, plane_at[CORE]]], axis=0)
            for a in range(taps)
            for h in range(2)
        ]
        combine = product(rows, w1, (ON, OWN, OFF))
        off_out[0, d] = combine((OFF, EDGE)).astype(off_out.dtype)
        start_off(OFF_1, d)
        on_out[0, d] = combine((ON, CORE))
        remote(ON_1, d).start()
        middle[d, EDGE] = combine((OWN, EDGE), (OFF, CORE))
        middle[d, CORE] = combine((OWN, CORE), (ON, EDGE))

    def finish_hidden(d):
        def store(kind, total):
            hidden[c, d + 1, plane_at[kind]] = jnp.maximum(total, 0.0).astype(hidden.dtype)

        await_off(OFF_1, d)
        store(EDGE, middle[d, EDGE] + off_in[0, d].astype(jnp.float32))
        remote(EDGE, d).start()
        remote(ON_1, d).wait_recv()
        store(CORE, middle[d, CORE] + on_in[0, d])

        @pl.when(d < EARLY)
        def _():
            remote(CORE, d).start()

    def first_step(t):
        @pl.when(t < depth)
        def _():
            remote(VOLUME, t).wait_recv()

        @pl.when(jnp.logical_and(t >= 1, t <= depth))
        def _():
            multiply_first(t - 1)

        @pl.when(t >= LAG)
        def _():
            finish_hidden(t - LAG)

    def plane_product(d, count, kind, roles):
        plane = plane_at[kind]
        rows = [
            jnp.concatenate([hidden[h, d + g + a, plane] for g in range(count)], axis=0)
            for a in range(taps)
            for h in range(2)
        ]
        return product(rows, w2, roles)

    def await_pair(kind, j):
        @pl.when(j == 0)
        def _():
            remote(kind, 0).wait_recv()

        remote(kind, 2 * j + 1).wait_recv()

        @pl.when(j < pairs - 1)
        def _():
            remote(kind, 2 * j + 2).wait_recv()

    def await_core(j):
        @pl.when(j == 0)
        def _():
            for d in range(EARLY):
                remote(CORE, d).wait_recv()

        @pl.when(jnp.logical_and(j > 0, j < pairs - 1))
        def _():
            remote(CORE, 2 * j + 1, 2).wait_recv()

        @pl.when(j == pairs - 1)
        def _():
            remote(CORE, depth - 1).wait_recv()

    def edge_step(j):
        await_pair(EDGE, j)
        combine = plane_product(2 * j, 2, EDGE, (ON, OWN, OFF))
        for g in range(2):
            off_out[1, 2 * j + g] = combine((OFF, g)).astype(off_out.dtype)
            start_off(OFF_2, 2 * j + g)
        for g in range(2):
            middle[2 * j + g, EDGE] = combine((OWN, g))
            middle[2 * j + g, CORE] = combine((ON, g))

    def core_sums(d, count, combine):
        for g in range(count):
            middle[d + g, CORE] = middle[d + g, CORE] + combine((OWN, g))
            middle[d + g, EDGE] = middle[d + g, EDGE] + combine((OFF, g))

    def core_send(d, count, combine):
        for g in range(count):
            on_out[1, d + g] = combine((ON, g))
            remote(ON_2, d + g).start()

    def core_step(j):
        await_core(j)
        combine = plane_product(2 * j, 2, CORE, (ON, OWN, OFF))
        core_send(2 * j, 2, combine)
        core_sums(2 * j, 2, combine)

    def core_end(count):
        d = depth - count
        for j in range(d // 2, pairs):
            await_core(jnp.int32(j))
        core_send(d, count, plane_product(d, count, CORE, (ON,)))

        @pl.when(s >= 0)
        def _():
            core_sums(d, count, plane_product(d, count, CORE, (OWN, OFF)))

    def finish(kind, j):
        plane = plane_at[kind]
        for g in range(2):
            d = 2 * j + g
            if kind == EDGE:
                await_off(OFF_2, d)
                other = off_in[1, d].astype(jnp.float32)
            else:
                remote(ON_2, d).wait_recv()
                other = on_in[1, d]
            total = middle[d, kind] + other + field[c, d + 1, plane].astype(jnp.float32)
            out[d, plane] = jnp.maximum(total, 0.0).astype(out.dtype)

    def all_sent(kind):
        if kind == VOLUME:
            whole_ref = volume
        elif kind in (EDGE, CORE):
            whole_ref = hidden.at[c, pl.ds(1, depth), plane_at[kind]]
        else:
            whole_ref = (off_out if kind in (OFF_1, OFF_2) else on_out).at[0 if kind in (OFF_1, ON_1) else 1]
        pltpu.make_async_copy(whole_ref, whole_ref, send_sem.at[kind]).wait()

    def drain(kinds, off_kind=None):
        for kind in kinds:
            all_sent(kind)
        if off_kind is not None:
            @pl.when(has_off)
            def _():
                all_sent(off_kind)

    own_copy.wait()
    pltpu.make_async_copy(w1, w1, local_sem.at[1]).wait()
    repeat(depth + LAG, first_step)
    repeat(pairs - 1, lambda j: remote(CORE, 2 * j + 1, 2).start(), first=1)
    remote(CORE, depth - 1).start()
    pltpu.make_async_copy(w2, w2, local_sem.at[2]).wait()
    drain((VOLUME, ON_1), OFF_1)

    whole = pairs - LATE

    def second_step(i):
        @pl.when(i != 1)
        def _():
            @pl.when(i <= pairs)
            def _():
                edge_step(jnp.maximum(i - 1, 0))

        @pl.when(jnp.logical_or(i == 1, i > pairs))
        def _():
            core_step(jnp.where(i == 1, 0, i - pairs))

    repeat(pairs + whole, second_step)
    for kind in (EDGE, CORE):
        repeat(whole, lambda j: finish(kind, j))
    core_end(2 * LATE)
    repeat(pairs, lambda j: finish(EDGE, j), first=whole)
    drain((EDGE, CORE), OFF_2)
    repeat(pairs, lambda j: finish(CORE, j), first=whole)
    drain((ON_2,))


def per_device(n_space, volume, first_filter, second_filter):
    depth, planes, width, half = volume.shape
    taps, _, _, in_c, out_c = first_filter.shape
    plane_buf = pltpu.VMEM((2, depth + 2, planes, width, half), jnp.bfloat16)
    off_buf = pltpu.VMEM((2, depth, width, out_c), jnp.bfloat16)
    on_buf = pltpu.VMEM((2, depth, width, out_c), jnp.float32)
    filter_buf = pltpu.VMEM((taps, in_c, 3 * taps * out_c), jnp.bfloat16)
    flops = 2 * 2 * 27 * depth * planes * width * in_c * out_c
    volume, first_filter, second_filter = (
        pltpu.with_memory_space_constraint(x, pltpu.HBM) for x in (volume, first_filter, second_filter)
    )
    return pl.pallas_call(
        functools.partial(kernel, n_space),
        out_shape=pltpu.VMEM(volume.shape, jnp.bfloat16),
        in_specs=[pl.BlockSpec(memory_space=pltpu.HBM)] * 3,
        out_specs=pl.BlockSpec(memory_space=pltpu.VMEM),
        scratch_shapes=[
            plane_buf,
            plane_buf,
            pltpu.VMEM((depth, planes, width, out_c), jnp.float32),
            off_buf,
            off_buf,
            on_buf,
            on_buf,
            filter_buf,
            filter_buf,
            pltpu.SemaphoreType.DMA((3,)),
            pltpu.SemaphoreType.DMA((7,)),
            pltpu.SemaphoreType.DMA((7, depth)),
        ],
        compiler_params=pltpu.CompilerParams(
            collective_id=0, has_side_effects=True, vmem_limit_bytes=40 << 20
        ),
        cost_estimate=pl.CostEstimate(
            flops=flops, bytes_accessed=4 * volume.size + 4 * first_filter.size, transcendentals=0
        ),
    )(volume, first_filter, second_filter)


def solution(mesh):
    return jax.shard_map(
        functools.partial(per_device, mesh.shape["space"]),
        mesh=mesh,
        in_specs=(
            P(None, "space", None, "chan"),
            P(None, None, None, None, "chan"),
            P(None, None, None, None, "chan"),
        ),
        out_specs=P(None, "space", None, "chan"),
        check_vma=False,
    )
```

```python
import functools

import jax
import jax.numpy as jnp
from jax import lax
from jax.experimental import pallas as pl
from jax.experimental.pallas import tpu as pltpu
from jax.sharding import PartitionSpec as P

MESH = pl.DeviceIdType.MESH
LAG = 4
EARLY = 3
LATE = 2
EDGE, CORE = range(2)
VOLUME, OFF_1, ON_1, OFF_2, ON_2 = range(2, 7)
ON, OWN, OFF = range(3)


def shifted(left, middle, right):
    width = middle.shape[0]
    at = lax.broadcasted_iota(jnp.int32, middle.shape, 0)
    left = jnp.where(at == 0, 0.0, pltpu.roll(left, 1, 0))
    right = jnp.where(at == width - 1, 0.0, pltpu.roll(right, width - 1, 0))
    return left + middle + right


def repeat(count, body, first=0):
    def step(i, carry):
        body(i)
        return carry

    lax.fori_loop(first, count, step, 0)


def kernel(
    n_space, volume, first, second, out,
    field, hidden, middle, off_out, off_in, on_out, on_in, w1, w2, local_sem, send_sem, recv_sem,
):
    s, c = lax.axis_index("space"), lax.axis_index("chan")
    depth, planes, width, half = volume.shape
    taps, out_c = first.shape[0], first.shape[4]
    pairs = depth // 2
    odd = lax.rem(s, 2)
    has_off = jnp.where(odd == 0, s > 0, s < n_space - 1)
    on_dev, off_dev, across = {"space": s + 1 - 2 * odd}, {"space": s - 1 + 2 * odd}, {"chan": 1 - c}
    plane_at = (odd, 1 - odd)
    tap_of = (2 * odd, 1, 2 - 2 * odd)

    barrier = pltpu.get_barrier_semaphore()
    pl.semaphore_signal(barrier, inc=1, device_id=across, device_id_type=MESH)
    pl.semaphore_signal(barrier, inc=1, device_id=on_dev, device_id_type=MESH)

    @pl.when(has_off)
    def _():
        pl.semaphore_signal(barrier, inc=1, device_id=off_dev, device_id_type=MESH)

    own_copy = pltpu.make_async_copy(volume, field.at[c, pl.ds(1, depth)], local_sem.at[0])
    own_copy.start()
    for k, (src, dst) in enumerate(((first, w1), (second, w2))):
        for role in range(3):
            for t in range(taps):
                col = role * taps + t
                pltpu.make_async_copy(
                    src.at[:, tap_of[role], t],
                    dst.at[:, :, pl.ds(col * out_c, out_c)],
                    local_sem.at[1 + k],
                ).start()

    rim = jnp.zeros((planes, width, half), field.dtype)
    for buf in (field, hidden):
        for h in range(2):
            buf[h, 0] = rim
            buf[h, depth + 1] = rim

    @pl.when(jnp.logical_not(has_off))
    def _():
        off_in[...] = jnp.zeros(off_in.shape, off_in.dtype)

    pl.semaphore_wait(barrier, 2 + has_off.astype(jnp.int32))

    def remote(kind, d, count=1):
        if kind == VOLUME:
            src, dst, dev = volume.at[d], field.at[c, d + 1], across
        elif kind in (EDGE, CORE):
            src = hidden.at[c, pl.ds(d + 1, count), plane_at[kind]]
            dst, dev = src, across
        elif kind == OFF_1:
            src, dst, dev = off_out.at[0, d], off_in.at[0, d], off_dev
        elif kind == OFF_2:
            src, dst, dev = off_out.at[1, pl.ds(2 * d, 2)], off_in.at[1, pl.ds(2 * d, 2)], off_dev
        else:
            k = 0 if kind == ON_1 else 1
            src, dst, dev = on_out.at[k, d], on_in.at[k, d], on_dev
        return pltpu.make_async_remote_copy(
            src_ref=src,
            dst_ref=dst,
            send_sem=send_sem.at[kind],
            recv_sem=recv_sem.at[kind, d],
            device_id=dev,
            device_id_type=MESH,
        )

    def start_off(kind, d):
        @pl.when(has_off)
        def _():
            remote(kind, d).start()

    def await_off(kind, d):
        @pl.when(has_off)
        def _():
            remote(kind, d).wait_recv()

    repeat(depth, lambda d: remote(VOLUME, d).start())

    def product(rows, w, roles):
        lhs = jnp.concatenate(rows, axis=1)
        per_role = taps * out_c
        cols = w[:, :, roles[0] * per_role : (roles[-1] + 1) * per_role]
        parts = jnp.dot(lhs, cols.reshape(lhs.shape[1], -1), preferred_element_type=jnp.float32)

        def combine(*terms):
            sums = []
            for t in range(taps):
                blocks = []
                for role, g in terms:
                    at = ((role - roles[0]) * taps + t) * out_c
                    blocks.append(parts[g * width : (g + 1) * width, at : at + out_c])
                sums.append(functools.reduce(jnp.add, blocks))
            return shifted(*sums)

        return combine

    def multiply_first(d):
        rows = [
            jnp.concatenate([field[h, d + a, plane_at[EDGE]], field[h, d + a, plane_at[CORE]]], axis=0)
            for a in range(taps)
            for h in range(2)
        ]
        combine = product(rows, w1, (ON, OWN, OFF))
        off_out[0, d] = combine((OFF, EDGE)).astype(off_out.dtype)
        start_off(OFF_1, d)
        on_out[0, d] = combine((ON, CORE))
        remote(ON_1, d).start()
        middle[d, EDGE] = combine((OWN, EDGE), (OFF, CORE))
        middle[d, CORE] = combine((OWN, CORE), (ON, EDGE))

    def finish_hidden(d):
        def store(kind, total):
            hidden[c, d + 1, plane_at[kind]] = jnp.maximum(total, 0.0).astype(hidden.dtype)

        await_off(OFF_1, d)
        store(EDGE, middle[d, EDGE] + off_in[0, d].astype(jnp.float32))
        remote(EDGE, d).start()
        remote(ON_1, d).wait_recv()
        store(CORE, middle[d, CORE] + on_in[0, d])

        @pl.when(d < EARLY)
        def _():
            remote(CORE, d).start()

    def first_step(t):
        @pl.when(t < depth)
        def _():
            remote(VOLUME, t).wait_recv()

        @pl.when(jnp.logical_and(t >= 1, t <= depth))
        def _():
            multiply_first(t - 1)

        @pl.when(t >= LAG)
        def _():
            finish_hidden(t - LAG)

    def plane_product(d, count, kind, roles):
        plane = plane_at[kind]
        rows = [
            jnp.concatenate([hidden[h, d + g + a, plane] for g in range(count)], axis=0)
            for a in range(taps)
            for h in range(2)
        ]
        return product(rows, w2, roles)

    def await_pair(kind, j):
        @pl.when(j == 0)
        def _():
            remote(kind, 0).wait_recv()

        remote(kind, 2 * j + 1).wait_recv()

        @pl.when(j < pairs - 1)
        def _():
            remote(kind, 2 * j + 2).wait_recv()

    def await_core(j):
        @pl.when(j == 0)
        def _():
            for d in range(EARLY):
                remote(CORE, d).wait_recv()

        @pl.when(jnp.logical_and(j > 0, j < pairs - 1))
        def _():
            remote(CORE, 2 * j + 1, 2).wait_recv()

        @pl.when(j == pairs - 1)
        def _():
            remote(CORE, depth - 1).wait_recv()

    def edge_step(j):
        await_pair(EDGE, j)
        combine = plane_product(2 * j, 2, EDGE, (ON, OWN, OFF))
        for g in range(2):
            off_out[1, 2 * j + g] = combine((OFF, g)).astype(off_out.dtype)
        start_off(OFF_2, j)
        for g in range(2):
            middle[2 * j + g, EDGE] = combine((OWN, g))
            middle[2 * j + g, CORE] = combine((ON, g))

    def core_sums(d, count, combine):
        for g in range(count):
            middle[d + g, CORE] = middle[d + g, CORE] + combine((OWN, g))
            middle[d + g, EDGE] = middle[d + g, EDGE] + combine((OFF, g))

    def core_send(d, count, combine):
        for g in range(count):
            on_out[1, d + g] = combine((ON, g))
            remote(ON_2, d + g).start()

    def core_step(j):
        await_core(j)
        combine = plane_product(2 * j, 2, CORE, (ON, OWN, OFF))
        core_send(2 * j, 2, combine)
        core_sums(2 * j, 2, combine)

    def core_end(count):
        d = depth - count
        for j in range(d // 2, pairs):
            await_core(jnp.int32(j))
        core_send(d, count, plane_product(d, count, CORE, (ON,)))

        @pl.when(s >= 0)
        def _():
            core_sums(d, count, plane_product(d, count, CORE, (OWN, OFF)))

    def finish(kind, j):
        plane = plane_at[kind]
        if kind == EDGE:
            await_off(OFF_2, j)
        for g in range(2):
            d = 2 * j + g
            if kind == EDGE:
                other = off_in[1, d].astype(jnp.float32)
            else:
                remote(ON_2, d).wait_recv()
                other = on_in[1, d]
            total = middle[d, kind] + other + field[c, d + 1, plane].astype(jnp.float32)
            out[d, plane] = jnp.maximum(total, 0.0).astype(out.dtype)

    def all_sent(kind):
        if kind == VOLUME:
            whole_ref = volume
        elif kind in (EDGE, CORE):
            whole_ref = hidden.at[c, pl.ds(1, depth), plane_at[kind]]
        else:
            whole_ref = (off_out if kind in (OFF_1, OFF_2) else on_out).at[0 if kind in (OFF_1, ON_1) else 1]
        pltpu.make_async_copy(whole_ref, whole_ref, send_sem.at[kind]).wait()

    def drain(kinds, off_kind=None):
        for kind in kinds:
            all_sent(kind)
        if off_kind is not None:
            @pl.when(has_off)
            def _():
                all_sent(off_kind)

    own_copy.wait()
    pltpu.make_async_copy(w1, w1, local_sem.at[1]).wait()
    repeat(depth + LAG, first_step)
    repeat(pairs - 1, lambda j: remote(CORE, 2 * j + 1, 2).start(), first=1)
    remote(CORE, depth - 1).start()
    pltpu.make_async_copy(w2, w2, local_sem.at[2]).wait()
    drain((VOLUME, ON_1), OFF_1)

    whole = pairs - LATE

    def second_step(i):
        @pl.when(i != 1)
        def _():
            @pl.when(i <= pairs)
            def _():
                edge_step(jnp.maximum(i - 1, 0))

        @pl.when(jnp.logical_or(i == 1, i > pairs))
        def _():
            core_step(jnp.where(i == 1, 0, i - pairs))

    repeat(pairs + whole, second_step)
    for kind in (EDGE, CORE):
        repeat(whole, lambda j: finish(kind, j))
    core_end(2 * LATE)
    repeat(pairs, lambda j: finish(EDGE, j), first=whole)
    drain((EDGE, CORE), OFF_2)
    repeat(pairs, lambda j: finish(CORE, j), first=whole)
    drain((ON_2,))


def per_device(n_space, volume, first_filter, second_filter):
    depth, planes, width, half = volume.shape
    taps, _, _, in_c, out_c = first_filter.shape
    plane_buf = pltpu.VMEM((2, depth + 2, planes, width, half), jnp.bfloat16)
    off_buf = pltpu.VMEM((2, depth, width, out_c), jnp.bfloat16)
    on_buf = pltpu.VMEM((2, depth, width, out_c), jnp.float32)
    filter_buf = pltpu.VMEM((taps, in_c, 3 * taps * out_c), jnp.bfloat16)
    flops = 2 * 2 * 27 * depth * planes * width * in_c * out_c
    volume, first_filter, second_filter = (
        pltpu.with_memory_space_constraint(x, pltpu.HBM) for x in (volume, first_filter, second_filter)
    )
    return pl.pallas_call(
        functools.partial(kernel, n_space),
        out_shape=pltpu.VMEM(volume.shape, jnp.bfloat16),
        in_specs=[pl.BlockSpec(memory_space=pltpu.HBM)] * 3,
        out_specs=pl.BlockSpec(memory_space=pltpu.VMEM),
        scratch_shapes=[
            plane_buf,
            plane_buf,
            pltpu.VMEM((depth, planes, width, out_c), jnp.float32),
            off_buf,
            off_buf,
            on_buf,
            on_buf,
            filter_buf,
            filter_buf,
            pltpu.SemaphoreType.DMA((3,)),
            pltpu.SemaphoreType.DMA((7,)),
            pltpu.SemaphoreType.DMA((7, depth)),
        ],
        compiler_params=pltpu.CompilerParams(
            collective_id=0, has_side_effects=True, vmem_limit_bytes=40 << 20
        ),
        cost_estimate=pl.CostEstimate(
            flops=flops, bytes_accessed=4 * volume.size + 4 * first_filter.size, transcendentals=0
        ),
    )(volume, first_filter, second_filter)


def solution(mesh):
    return jax.shard_map(
        functools.partial(per_device, mesh.shape["space"]),
        mesh=mesh,
        in_specs=(
            P(None, "space", None, "chan"),
            P(None, None, None, None, "chan"),
            P(None, None, None, None, "chan"),
        ),
        out_specs=P(None, "space", None, "chan"),
        check_vma=False,
    )
```

```python
import functools

import jax
import jax.numpy as jnp
from jax import lax
from jax.experimental import pallas as pl
from jax.experimental.pallas import tpu as pltpu
from jax.sharding import PartitionSpec as P

MESH = pl.DeviceIdType.MESH
LAG = 4
EARLY = 3
LATE = 2
EDGE, CORE = range(2)
VOLUME, OFF_1, ON_1, OFF_2, ON_2 = range(2, 7)
ON, OWN, OFF = range(3)


def shifted(left, middle, right):
    width = middle.shape[0]
    at = lax.broadcasted_iota(jnp.int32, middle.shape, 0)
    left = jnp.where(at == 0, 0.0, pltpu.roll(left, 1, 0))
    right = jnp.where(at == width - 1, 0.0, pltpu.roll(right, width - 1, 0))
    return left + middle + right


def repeat(count, body, first=0):
    def step(i, carry):
        body(i)
        return carry

    lax.fori_loop(first, count, step, 0)


def kernel(
    n_space, volume, first, second, out,
    field, hidden, middle, off_out, off_in, on_out, on_in, w1, w2, local_sem, send_sem, recv_sem,
):
    s, c = lax.axis_index("space"), lax.axis_index("chan")
    depth, planes, width, half = volume.shape
    taps, out_c = first.shape[0], first.shape[4]
    pairs = depth // 2
    odd = lax.rem(s, 2)
    has_off = jnp.where(odd == 0, s > 0, s < n_space - 1)
    on_dev, off_dev, across = {"space": s + 1 - 2 * odd}, {"space": s - 1 + 2 * odd}, {"chan": 1 - c}
    plane_at = (odd, 1 - odd)
    tap_of = (2 * odd, 1, 2 - 2 * odd)

    barrier = pltpu.get_barrier_semaphore()
    pl.semaphore_signal(barrier, inc=1, device_id=across, device_id_type=MESH)
    pl.semaphore_signal(barrier, inc=1, device_id=on_dev, device_id_type=MESH)

    @pl.when(has_off)
    def _():
        pl.semaphore_signal(barrier, inc=1, device_id=off_dev, device_id_type=MESH)

    own_copy = pltpu.make_async_copy(volume, field.at[c, pl.ds(1, depth)], local_sem.at[0])
    own_copy.start()
    for k, (src, dst) in enumerate(((first, w1), (second, w2))):
        for role in range(3):
            for t in range(taps):
                col = role * taps + t
                pltpu.make_async_copy(
                    src.at[:, tap_of[role], t],
                    dst.at[:, :, pl.ds(col * out_c, out_c)],
                    local_sem.at[1 + k],
                ).start()

    rim = jnp.zeros((planes, width, half), field.dtype)
    for buf in (field, hidden):
        for h in range(2):
            buf[h, 0] = rim
            buf[h, depth + 1] = rim

    @pl.when(jnp.logical_not(has_off))
    def _():
        off_in[...] = jnp.zeros(off_in.shape, off_in.dtype)

    pl.semaphore_wait(barrier, 2 + has_off.astype(jnp.int32))

    def remote(kind, d, count=1):
        if kind == VOLUME:
            src, dst, dev = volume.at[d], field.at[c, d + 1], across
        elif kind in (EDGE, CORE):
            src = hidden.at[c, pl.ds(d + 1, count), plane_at[kind]]
            dst, dev = src, across
        elif kind in (OFF_1, OFF_2):
            k = 0 if kind == OFF_1 else 1
            src, dst, dev = off_out.at[k, d], off_in.at[k, d], off_dev
        else:
            k = 0 if kind == ON_1 else 1
            src, dst, dev = on_out.at[k, d], on_in.at[k, d], on_dev
        return pltpu.make_async_remote_copy(
            src_ref=src,
            dst_ref=dst,
            send_sem=send_sem.at[kind],
            recv_sem=recv_sem.at[kind, d],
            device_id=dev,
            device_id_type=MESH,
        )

    def start_off(kind, d):
        @pl.when(has_off)
        def _():
            remote(kind, d).start()

    def await_off(kind, d):
        @pl.when(has_off)
        def _():
            remote(kind, d).wait_recv()

    repeat(depth, lambda d: remote(VOLUME, d).start())

    def product(rows, w, roles):
        lhs = jnp.concatenate(rows, axis=1)
        per_role = taps * out_c
        cols = w[:, :, roles[0] * per_role : (roles[-1] + 1) * per_role]
        parts = jnp.dot(lhs, cols.reshape(lhs.shape[1], -1), preferred_element_type=jnp.float32)

        def combine(*terms):
            sums = []
            for t in range(taps):
                blocks = []
                for role, g in terms:
                    at = ((role - roles[0]) * taps + t) * out_c
                    blocks.append(parts[g * width : (g + 1) * width, at : at + out_c])
                sums.append(functools.reduce(jnp.add, blocks))
            return shifted(*sums)

        return combine

    def multiply_first(d):
        rows = [
            jnp.concatenate([field[h, d + a, plane_at[EDGE]], field[h, d + a, plane_at[CORE]]], axis=0)
            for a in range(taps)
            for h in range(2)
        ]
        combine = product(rows, w1, (ON, OWN, OFF))
        off_out[0, d] = combine((OFF, EDGE)).astype(off_out.dtype)
        start_off(OFF_1, d)
        on_out[0, d] = combine((ON, CORE))
        remote(ON_1, d).start()
        middle[d, EDGE] = combine((OWN, EDGE), (OFF, CORE))
        middle[d, CORE] = combine((OWN, CORE), (ON, EDGE))

    def finish_hidden(d):
        def store(kind, total):
            hidden[c, d + 1, plane_at[kind]] = jnp.maximum(total, 0.0).astype(hidden.dtype)

        await_off(OFF_1, d)
        store(EDGE, middle[d, EDGE] + off_in[0, d].astype(jnp.float32))
        remote(EDGE, d).start()
        remote(ON_1, d).wait_recv()
        store(CORE, middle[d, CORE] + on_in[0, d])

        @pl.when(d < EARLY)
        def _():
            remote(CORE, d).start()

    def first_step(t):
        @pl.when(t < depth)
        def _():
            remote(VOLUME, t).wait_recv()

        @pl.when(jnp.logical_and(t >= 1, t <= depth))
        def _():
            multiply_first(t - 1)

        @pl.when(t >= LAG)
        def _():
            finish_hidden(t - LAG)

    def plane_product(d, count, kind, roles):
        plane = plane_at[kind]
        rows = [
            jnp.concatenate([hidden[h, d + g + a, plane] for g in range(count)], axis=0)
            for a in range(taps)
            for h in range(2)
        ]
        return product(rows, w2, roles)

    def await_pair(kind, j):
        @pl.when(j == 0)
        def _():
            remote(kind, 0).wait_recv()

        remote(kind, 2 * j + 1).wait_recv()

        @pl.when(j < pairs - 1)
        def _():
            remote(kind, 2 * j + 2).wait_recv()

    def await_core(j):
        @pl.when(j == 0)
        def _():
            for d in range(EARLY):
                remote(CORE, d).wait_recv()

        @pl.when(jnp.logical_and(j > 0, j < pairs - 1))
        def _():
            remote(CORE, 2 * j + 1, 2).wait_recv()

        @pl.when(j == pairs - 1)
        def _():
            remote(CORE, depth - 1).wait_recv()

    def edge_step(j):
        await_pair(EDGE, j)
        combine = plane_product(2 * j, 2, EDGE, (ON, OWN, OFF))
        for g in range(2):
            off_out[1, 2 * j + g] = combine((OFF, g)).astype(off_out.dtype)
            start_off(OFF_2, 2 * j + g)
        for g in range(2):
            middle[2 * j + g, EDGE] = combine((OWN, g))
            middle[2 * j + g, CORE] = combine((ON, g))

    def core_sums(d, count, combine):
        for g in range(count):
            middle[d + g, CORE] = middle[d + g, CORE] + combine((OWN, g))
            middle[d + g, EDGE] = middle[d + g, EDGE] + combine((OFF, g))

    def core_send(d, count, combine):
        for g in range(count):
            on_out[1, d + g] = combine((ON, g))
            remote(ON_2, d + g).start()

    def core_step(j):
        await_core(j)
        combine = plane_product(2 * j, 2, CORE, (ON, OWN, OFF))
        core_send(2 * j, 2, combine)
        core_sums(2 * j, 2, combine)

    def core_end(count):
        d = depth - count
        for j in range(d // 2, pairs):
            await_core(jnp.int32(j))
        core_send(d, count, plane_product(d, count, CORE, (ON,)))

        @pl.when(s >= 0)
        def _():
            core_sums(d, count, plane_product(d, count, CORE, (OWN, OFF)))

    def finish(kind, j):
        plane = plane_at[kind]
        for g in range(2):
            d = 2 * j + g
            if kind == EDGE:
                await_off(OFF_2, d)
                other = off_in[1, d].astype(jnp.float32)
            else:
                remote(ON_2, d).wait_recv()
                other = on_in[1, d]
            total = middle[d, kind] + other + field[c, d + 1, plane].astype(jnp.float32)
            out[d, plane] = jnp.maximum(total, 0.0).astype(out.dtype)

    def all_sent(kind):
        if kind == VOLUME:
            whole_ref = volume
        elif kind in (EDGE, CORE):
            whole_ref = hidden.at[c, pl.ds(1, depth), plane_at[kind]]
        else:
            whole_ref = (off_out if kind in (OFF_1, OFF_2) else on_out).at[0 if kind in (OFF_1, ON_1) else 1]
        pltpu.make_async_copy(whole_ref, whole_ref, send_sem.at[kind]).wait()

    def drain(kinds, off_kind=None):
        for kind in kinds:
            all_sent(kind)
        if off_kind is not None:
            @pl.when(has_off)
            def _():
                all_sent(off_kind)

    own_copy.wait()
    pltpu.make_async_copy(w1, w1, local_sem.at[1]).wait()
    repeat(depth + LAG, first_step)
    repeat(pairs - 1, lambda j: remote(CORE, 2 * j + 1, 2).start(), first=1)
    remote(CORE, depth - 1).start()
    pltpu.make_async_copy(w2, w2, local_sem.at[2]).wait()
    drain((VOLUME, ON_1), OFF_1)

    whole = pairs - LATE

    def second_step(i):
        @pl.when(i != 1)
        def _():
            @pl.when(i <= pairs)
            def _():
                edge_step(jnp.maximum(i - 1, 0))

        @pl.when(jnp.logical_or(i == 1, i > pairs))
        def _():
            core_step(jnp.where(i == 1, 0, i - pairs))

    repeat(pairs + whole, second_step)
    for kind in (EDGE, CORE):
        repeat(whole, lambda j: finish(kind, j))
    core_end(2 * LATE)
    for j in range(whole, pairs):
        finish(EDGE, j)
    drain((EDGE, CORE), OFF_2)
    for j in range(whole, pairs):
        finish(CORE, j)
    drain((ON_2,))


def per_device(n_space, volume, first_filter, second_filter):
    depth, planes, width, half = volume.shape
    taps, _, _, in_c, out_c = first_filter.shape
    plane_buf = pltpu.VMEM((2, depth + 2, planes, width, half), jnp.bfloat16)
    off_buf = pltpu.VMEM((2, depth, width, out_c), jnp.bfloat16)
    on_buf = pltpu.VMEM((2, depth, width, out_c), jnp.float32)
    filter_buf = pltpu.VMEM((taps, in_c, 3 * taps * out_c), jnp.bfloat16)
    flops = 2 * 2 * 27 * depth * planes * width * in_c * out_c
    volume, first_filter, second_filter = (
        pltpu.with_memory_space_constraint(x, pltpu.HBM) for x in (volume, first_filter, second_filter)
    )
    return pl.pallas_call(
        functools.partial(kernel, n_space),
        out_shape=pltpu.VMEM(volume.shape, jnp.bfloat16),
        in_specs=[pl.BlockSpec(memory_space=pltpu.HBM)] * 3,
        out_specs=pl.BlockSpec(memory_space=pltpu.VMEM),
        scratch_shapes=[
            plane_buf,
            plane_buf,
            pltpu.VMEM((depth, planes, width, out_c), jnp.float32),
            off_buf,
            off_buf,
            on_buf,
            on_buf,
            filter_buf,
            filter_buf,
            pltpu.SemaphoreType.DMA((3,)),
            pltpu.SemaphoreType.DMA((7,)),
            pltpu.SemaphoreType.DMA((7, depth)),
        ],
        compiler_params=pltpu.CompilerParams(
            collective_id=0, has_side_effects=True, vmem_limit_bytes=40 << 20
        ),
        cost_estimate=pl.CostEstimate(
            flops=flops, bytes_accessed=4 * volume.size + 4 * first_filter.size, transcendentals=0
        ),
    )(volume, first_filter, second_filter)


def solution(mesh):
    return jax.shard_map(
        functools.partial(per_device, mesh.shape["space"]),
        mesh=mesh,
        in_specs=(
            P(None, "space", None, "chan"),
            P(None, None, None, None, "chan"),
            P(None, None, None, None, "chan"),
        ),
        out_specs=P(None, "space", None, "chan"),
        check_vma=False,
    )
```
